256 devices in a mesh: section: 8 (over x, y_lo), dp: 32 (over z, y_hi, core).
Axes of the slice: x: 4, y: 4 (y_hi: 2, y_lo: 2; y = y_hi * 2 + y_lo), z: 8, core: 2. Of those that a mesh axis runs over, the one named last changes fastest.
Arguments:
- acts: bfloat16 [8, 9, 128, 32, 128], P('section', None, 'dp'), may hold values from -6 to 6
- kernels: bfloat16 [8, 3, 3, 3, 128, 128], P('section'), may hold values from -0.078125 to 0.078125
- cotangent: bfloat16 [9, 128, 32, 128], P(None, 'dp'), may hold values from -6 to 6
Outputs:
- input_grads: bfloat16 [8, 9, 128, 32, 128], P('section', None, 'dp')
- kernel_grads: float32 [8, 128, 27, 128], P('section', 'dp')
The draws below stay inside these ranges and needn't reach their ends.
All inputs are finite; a program needn't handle non-finite values.
Results may differ from the reference program's by a relative error of at most 0.03.
Values may be sent and summed in bfloat16 or wider, within the bound.
No kernel may reach another device: no remote copies, remote signals or barrier semaphores. Data moves between devices by JAX's collectives and lax.ppermute only.
A program may use at most 128 MiB of HBM per device.

```python
import math
import jax
import jax.numpy as jnp
from jax import lax

C = 128
F = 9
WIN = 32
H = 128
SECTIONS = 8


def raised(values, stream_key, source, target, parts, factor):
    def block_of(axis_at):
        return (jnp.arange(values.shape[axis_at]) // (values.shape[axis_at] // parts)).reshape((-1,) + (1,) * (values.ndim - 1 - axis_at))

    one_side = jax.random.permutation(stream_key, parts)[block_of(target)]
    other_side = (block_of(target) + parts // 2) % parts
    return jnp.where((block_of(source) == one_side) | (block_of(source) == other_side), factor * values, values)


def level_of(key, extent, shards, low, high):
    factor_of = 1.0
    for axis_at, blocks in shards:
        heights = jax.random.uniform(jax.random.fold_in(jax.random.fold_in(key, 6), axis_at), (blocks,), jnp.float32, low / len(shards), high / len(shards))
        factor_of = factor_of * jnp.repeat(jnp.exp(heights), extent[axis_at] // blocks).reshape((-1,) + (1,) * (len(extent) - 1 - axis_at))
    return factor_of


def normal_values(stream_key, dims, scale, reach, pieces=(), held_as=jnp.bfloat16):
    drawn = scale * jax.random.normal(stream_key, dims, jnp.float32)
    if pieces:
        drawn = drawn * level_of(stream_key, dims, pieces, -0.22, 0.18)
    return jnp.clip(drawn, -reach, reach).astype(held_as)


def heavy_noise(own_key, extent, deviation, reach, cuts, heavy, kind=jnp.bfloat16):
    result = deviation * jax.random.normal(own_key, extent, jnp.float32)
    if cuts:
        result = result * level_of(own_key, extent, cuts, -0.22, 0.18)
    return jnp.clip(raised(result, jax.random.fold_in(own_key, 3), *heavy), -reach, reach).astype(kind)


def setup_inputs(seed: int = 0) -> dict:
    seeds = jax.random.split(jax.random.key(seed), 4)
    acts = heavy_noise(seeds[0], (SECTIONS, F, H, WIN, C), 1.0, 6.0, ((0, 8), (2, 32)), (2, 4, 32, 2.75))
    kernels = normal_values(seeds[1], (SECTIONS, 3, 3, 3, C, C), (54 * C) ** -0.5, 0.078125, ((0, 8),))
    cotangent = normal_values(seeds[2], (F, H, WIN, C), 1.0, 6.0, ((1, 32),))
    return {"acts": acts, "kernels": kernels, "cotangent": cotangent}


def back_conv(kern, grad):
    flipped = jnp.swapaxes(kern[::-1, ::-1, ::-1], 3, 4)
    out = lax.conv_general_dilated(grad[None], flipped, (1, 1, 1), ((0, 2), (1, 1), (1, 1)), dimension_numbers=('NDHWC', 'DHWIO', 'NDHWC'), preferred_element_type=jnp.float32)
    return out[0]

def kernel_term(upad, grad):
    flat = grad.reshape(-1, grad.shape[-1])
    terms = []
    for i in range(3):
        for j in range(3):
            for k in range(3):
                sliced = upad[i:i + F, j:j + H, k:k + WIN].reshape(-1, upad.shape[-1])
                terms.append(jnp.dot(sliced.T, flat, preferred_element_type=jnp.float32))
    return jnp.stack(terms, axis=1)

def reference(acts, kernels, cotangent):
    scale = 1.0 / math.sqrt(F * H * WIN)
    grad = cotangent
    grads_out = []
    kernel_out = []
    for section_id in range(SECTIONS - 1, -1, -1):
        xval = acts[section_id].astype(jnp.float32)
        sig = jax.nn.sigmoid(xval)
        slope = sig * (1.0 + xval * (1.0 - sig))
        back = back_conv(kernels[section_id], grad)
        new_grad = (grad.astype(jnp.float32) + slope * back).astype(jnp.bfloat16)
        activ = (xval * sig).astype(jnp.bfloat16)
        upad = jnp.pad(activ, ((2, 0), (1, 1), (1, 1), (0, 0)))
        kernel_out.append(kernel_term(upad, grad) * scale)
        grads_out.append(new_grad)
        grad = new_grad
    return (jnp.stack(grads_out[::-1], axis=0), jnp.stack(kernel_out[::-1], axis=0))
```

```python
import functools
import math

import jax
import jax.numpy as jnp
import numpy as np
from jax import lax
from jax.experimental import pallas as pl
from jax.experimental.pallas import tpu as pltpu
from jax.sharding import PartitionSpec as P

BF = jnp.bfloat16
F32 = jnp.float32
DP = 32
SEC = 8
FRAMES = 9
ROWS = 4
COLS = 32
CH = 128
AXES = ("section", "dp")
HALVING = (1, 2, 4, 8, 16)


def permute(value, hops):
    pairs = [
        (src * DP + d, dst * DP + d + off)
        for src, dst, off in hops
        for d in range(DP)
        if 0 <= d + off < DP
    ]
    return lax.ppermute(value, AXES, pairs)


def fill(x_ref, frame, row, value):
    count = value.shape[0] // COLS
    col = lax.broadcasted_iota(jnp.int32, value.shape, 0) % COLS
    size = value.shape[0]
    after = jnp.where(col == COLS - 1, 0.0, pltpu.roll(value, size - 1, 0))
    before = jnp.where(col == 0, 0.0, pltpu.roll(value, 1, 0))
    for n, part in enumerate((after, value, before)):
        x_ref[frame, row : row + count, :, n * CH : (n + 1) * CH] = part.astype(BF).reshape(
            count, COLS, CH
        )


def back_pass(x_ref, w_ref, slope_ref, rows, emit):
    group = 3
    size = rows * COLS
    one_later = None
    two_later = None
    for start in range(FRAMES - group, -1, -group):
        lhs = jnp.concatenate(
            [x_ref[start : start + group, 2 - j : 2 - j + rows] for j in range(3)], axis=-1
        ).reshape(group * size, 9 * CH)
        part = jnp.dot(lhs, w_ref[...], preferred_element_type=F32)
        for t in range(group - 1, -1, -1):
            here = part[t * size : (t + 1) * size]
            back = here[:, 2 * CH :]
            if one_later is not None:
                back = back + one_later[:, CH : 2 * CH]
            if two_later is not None:
                back = back + two_later[:, :CH]
            frame = start + t
            grad = x_ref[frame, 1 : 1 + rows, :, CH : 2 * CH].reshape(size, CH).astype(F32)
            new = grad + slope_ref[frame].reshape(size, CH) * back
            emit(frame, new.astype(BF))
            two_later = one_later
            one_later = here


def single_kernel(low_ref, own_ref, high_ref, w_ref, slope_ref, out_ref, x_ref):
    for t in range(FRAMES):
        whole = jnp.concatenate([low_ref[t], own_ref[t], high_ref[t]], axis=0)
        fill(x_ref, t, 0, whole.reshape(-1, CH).astype(F32))

    def emit(frame, value):
        out_ref[frame] = value.reshape(ROWS, COLS, CH)

    back_pass(x_ref, w_ref, slope_ref, ROWS, emit)


def double_kernel(
    low_ref, own_ref, high_ref, w1_ref, slope1_ref, w0_ref, slope0_ref, out_ref, x1_ref, x0_ref
):
    for t in range(FRAMES):
        whole = jnp.concatenate([low_ref[t], own_ref[t], high_ref[t]], axis=0)
        fill(x1_ref, t, 0, whole.reshape(-1, CH).astype(F32))

    def emit_mid(frame, value):
        fill(x0_ref, frame, 0, value.astype(F32))

    def emit(frame, value):
        out_ref[frame] = value.reshape(ROWS, COLS, CH)

    back_pass(x1_ref, w1_ref, slope1_ref, ROWS + 2, emit_mid)
    back_pass(x0_ref, w0_ref, slope0_ref, ROWS, emit)


def in_vmem(count):
    return [pl.BlockSpec(memory_space=pltpu.VMEM)] * count


def single(low, own, high, w, slope):
    return pl.pallas_call(
        single_kernel,
        out_shape=jax.ShapeDtypeStruct((FRAMES, ROWS, COLS, CH), BF),
        in_specs=in_vmem(5),
        out_specs=pl.BlockSpec(memory_space=pltpu.VMEM),
        scratch_shapes=[pltpu.VMEM((FRAMES, ROWS + 2, COLS, 3 * CH), BF)],
        compiler_params=pltpu.CompilerParams(vmem_limit_bytes=24 << 20),
        name="one_block",
    )(low, own, high, w, slope)


def double(low, own, high, w1, slope1, w0, slope0):
    return pl.pallas_call(
        double_kernel,
        out_shape=jax.ShapeDtypeStruct((FRAMES, ROWS, COLS, CH), BF),
        in_specs=in_vmem(7),
        out_specs=pl.BlockSpec(memory_space=pltpu.VMEM),
        scratch_shapes=[
            pltpu.VMEM((FRAMES, ROWS + 4, COLS, 3 * CH), BF),
            pltpu.VMEM((FRAMES, ROWS + 2, COLS, 3 * CH), BF),
        ],
        compiler_params=pltpu.CompilerParams(vmem_limit_bytes=24 << 20),
        name="two_blocks",
    )(low, own, high, w1, slope1, w0, slope0)


def taps_kernel(scale, ut_ref, g_ref, out_ref):
    grad = g_ref[...].reshape(FRAMES, ROWS * COLS, CH)
    padded = jnp.concatenate([grad, jnp.zeros((2, ROWS * COLS, CH), BF)], axis=0)
    rhs = jnp.concatenate([padded[2 - i : 2 - i + FRAMES] for i in range(3)], axis=-1).reshape(
        FRAMES * ROWS * COLS, 3 * CH
    )
    step = 3 * CH
    for n in range(3):
        rows = slice(n * step, (n + 1) * step)
        part = jnp.dot(ut_ref[rows, :], rhs, preferred_element_type=F32)
        out_ref[rows, :] = (part * scale).astype(BF)


def taps(ut, grad, scale):
    return pl.pallas_call(
        functools.partial(taps_kernel, scale),
        out_shape=jax.ShapeDtypeStruct((9 * CH, 3 * CH), BF),
        in_specs=in_vmem(2),
        out_specs=pl.BlockSpec(memory_space=pltpu.VMEM),
        compiler_params=pltpu.CompilerParams(vmem_limit_bytes=24 << 20),
        name="kernel_taps",
    )(ut, grad)


def channel_order():
    share = CH // DP
    order = []
    for n in range(CH):
        slot, rest = divmod(n, share)
        d = 0
        for place, bit in enumerate(HALVING):
            if (slot >> (len(HALVING) - 1 - place)) & 1:
                d |= bit
        order.append(d * share + rest)
    matrix = np.zeros((CH, CH), np.float32)
    matrix[np.arange(CH), order] = 1.0
    return matrix


def slope_of(x):
    x = x.astype(F32)
    sig = jax.nn.sigmoid(x)
    return sig * (1.0 + x * (1.0 - sig))


def as_matrix(kern):
    return jnp.transpose(kern, (1, 2, 4, 0, 3)).reshape(9 * CH, 3 * CH)


def local(acts, kernels, cotangent):
    me = lax.axis_index("section")
    dp = lax.axis_index("dp")
    scale = 1.0 / math.sqrt(FRAMES * ROWS * DP * COLS)
    own_acts = acts[0]
    odd = [s for s in range(SEC) if s % 2 == 1]
    every = range(SEC)

    low0 = permute(cotangent[:, -1:], [(7, 7, 1)])
    high0 = permute(cotangent[:, :1], [(7, 7, -1)])
    kern_next = permute(kernels[0], [(s + 1, s, 0) for s in odd[:-1]])
    act_low = permute(own_acts[:, -1:], [(s, s, 1) for s in every])
    act_high = permute(own_acts[:, :1], [(s, s, -1) for s in every])
    act6 = jnp.concatenate([act_low, own_acts, act_high], axis=1)
    act_next = permute(act6, [(s + 1, s, 0) for s in odd[:-1]])
    act_prev = permute(act6, [(s, (s + 1) % SEC, 0) for s in every])

    w = as_matrix(kernels[0])
    w_next = as_matrix(kern_next)
    slope = slope_of(own_acts)
    row = lax.broadcasted_iota(jnp.int32, act_next.shape, 1) + dp * ROWS - 1
    inside = (row >= 0) & (row < DP * ROWS)
    slope_next = jnp.where(inside, slope_of(act_next), 0.0)

    x_prev = act_prev.astype(F32)
    u = jnp.pad(
        (x_prev * jax.nn.sigmoid(x_prev)).astype(BF), ((0, 0), (0, 0), (1, 1), (0, 0))
    )
    shifted = jnp.stack(
        [
            u[:, j : j + ROWS, k : k + COLS].reshape(-1, CH)
            for j in range(3)
            for k in range(3)
        ]
    )
    picked = lax.dot_general(
        jnp.asarray(channel_order(), BF),
        shifted,
        (((1,), (2,)), ((), ())),
        preferred_element_type=F32,
    ).astype(BF)
    ut = picked.reshape(9 * CH, FRAMES * ROWS * COLS)

    result = lax.cond(
        me == 7,
        lambda: single(low0, cotangent, high0, w, slope),
        lambda: jnp.zeros_like(cotangent),
    )
    for s in (5, 3, 1):
        own = permute(result, [(s + 2, s, 0)])
        low = permute(result[:, 2:], [(s + 2, s, 1)])
        high = permute(result[:, :2], [(s + 2, s, -1)])
        result = lax.cond(
            me == s,
            lambda low=low, own=own, high=high: double(
                low, own, high, w_next, slope_next, w, slope
            ),
            lambda result=result: result,
        )

    def even(result, sections):
        hops = [(s + 1, s) for s in sections]
        own = permute(result, [(a, b, 0) for a, b in hops])
        low = permute(result[:, -1:], [(a, b, 1) for a, b in hops])
        high = permute(result[:, :1], [(a, b, -1) for a, b in hops])
        live = functools.reduce(jnp.logical_or, [me == s for s in sections])
        return lax.cond(
            live,
            lambda: single(low, own, high, w, slope),
            lambda: result,
        )

    result = even(result, (6, 4, 2))
    final = even(result, (0,))

    grad = jnp.where(me == 0, cotangent, result)
    part = taps(ut, grad, scale)
    for bit in HALVING:
        half = part.shape[0] // 2
        mine = (dp // bit) % 2
        keep = lax.dynamic_slice_in_dim(part, mine * half, half, 0)
        give = lax.dynamic_slice_in_dim(part, (1 - mine) * half, half, 0)
        got = lax.ppermute(
            give, AXES, [(s * DP + d, s * DP + (d ^ bit)) for s in every for d in range(DP)]
        )
        part = (keep.astype(F32) + got.astype(F32)).astype(BF)
    part = permute(part, [((s + 1) % SEC, s, 0) for s in every]).astype(F32)
    share = CH // DP
    kernel_part = jnp.transpose(part.reshape(share, 9, 3, CH), (0, 2, 1, 3)).reshape(share, 27, CH)
    return (final[None], kernel_part[None])


def solution(mesh):
    return jax.shard_map(
        local,
        mesh=mesh,
        in_specs=(
            P("section", None, "dp", None, None),
            P("section", None, None, None, None, None),
            P(None, "dp", None, None),
        ),
        out_specs=(P("section", None, "dp", None, None), P("section", "dp", None, None)),
        check_vma=False,
    )
```

```python
import functools
import math

import jax
import jax.numpy as jnp
import numpy as np
from jax import lax
from jax.experimental import pallas as pl
from jax.experimental.pallas import tpu as pltpu
from jax.sharding import PartitionSpec as P

BF = jnp.bfloat16
F32 = jnp.float32
DP = 32
SEC = 8
FRAMES = 9
ROWS = 4
COLS = 32
CH = 128
AXES = ("section", "dp")
HALVING = (1, 2, 4, 8, 16)


def permute(value, hops):
    pairs = [
        (src * DP + d, dst * DP + d + off)
        for src, dst, off in hops
        for d in range(DP)
        if 0 <= d + off < DP
    ]
    return lax.ppermute(value, AXES, pairs)


def fill(x_ref, frame, row, value):
    count = value.shape[0] // COLS
    col = lax.broadcasted_iota(jnp.int32, value.shape, 0) % COLS
    size = value.shape[0]
    after = jnp.where(col == COLS - 1, 0.0, pltpu.roll(value, size - 1, 0))
    before = jnp.where(col == 0, 0.0, pltpu.roll(value, 1, 0))
    for n, part in enumerate((after, value, before)):
        x_ref[frame, row : row + count, :, n * CH : (n + 1) * CH] = part.astype(BF).reshape(
            count, COLS, CH
        )


def back_pass(x_ref, w_ref, slope_ref, rows, emit):
    group = 3
    size = rows * COLS
    one_later = None
    two_later = None
    for start in range(FRAMES - group, -1, -group):
        lhs = jnp.concatenate(
            [x_ref[start : start + group, 2 - j : 2 - j + rows] for j in range(3)], axis=-1
        ).reshape(group * size, 9 * CH)
        part = jnp.dot(lhs, w_ref[...], preferred_element_type=F32)
        for t in range(group - 1, -1, -1):
            here = part[t * size : (t + 1) * size]
            back = here[:, 2 * CH :]
            if one_later is not None:
                back = back + one_later[:, CH : 2 * CH]
            if two_later is not None:
                back = back + two_later[:, :CH]
            frame = start + t
            grad = x_ref[frame, 1 : 1 + rows, :, CH : 2 * CH].reshape(size, CH).astype(F32)
            new = grad + slope_ref[frame].reshape(size, CH) * back
            emit(frame, new.astype(BF))
            two_later = one_later
            one_later = here


def emit_to(refs):
    out_ref, top_ref, bottom_ref = refs

    def emit(frame, value):
        whole = value.reshape(ROWS, COLS, CH)
        out_ref[frame] = whole
        top_ref[frame] = whole[:2]
        bottom_ref[frame] = whole[2:]

    return emit


def single_kernel(low_ref, own_ref, high_ref, w_ref, slope_ref, *rest):
    *outs, x_ref = rest
    for t in range(FRAMES):
        whole = jnp.concatenate([low_ref[t], own_ref[t], high_ref[t]], axis=0)
        fill(x_ref, t, 0, whole.reshape(-1, CH).astype(F32))
    back_pass(x_ref, w_ref, slope_ref, ROWS, emit_to(outs))


def double_kernel(low_ref, own_ref, high_ref, w1_ref, slope1_ref, w0_ref, slope0_ref, *rest):
    *outs, x1_ref, x0_ref = rest
    for t in range(FRAMES):
        whole = jnp.concatenate([low_ref[t], own_ref[t], high_ref[t]], axis=0)
        fill(x1_ref, t, 0, whole.reshape(-1, CH).astype(F32))

    def emit_mid(frame, value):
        fill(x0_ref, frame, 0, value.astype(F32))

    back_pass(x1_ref, w1_ref, slope1_ref, ROWS + 2, emit_mid)
    back_pass(x0_ref, w0_ref, slope0_ref, ROWS, emit_to(outs))


def in_vmem(count):
    return [pl.BlockSpec(memory_space=pltpu.VMEM)] * count


def gradient_shapes():
    return [
        jax.ShapeDtypeStruct((FRAMES, rows, COLS, CH), BF) for rows in (ROWS, 2, 2)
    ]


def single(low, own, high, w, slope):
    return pl.pallas_call(
        single_kernel,
        out_shape=gradient_shapes(),
        in_specs=in_vmem(5),
        out_specs=in_vmem(3),
        scratch_shapes=[pltpu.VMEM((FRAMES, ROWS + 2, COLS, 3 * CH), BF)],
        compiler_params=pltpu.CompilerParams(vmem_limit_bytes=24 << 20),
        name="one_block",
    )(low, own, high, w, slope)


def double(low, own, high, w1, slope1, w0, slope0):
    return pl.pallas_call(
        double_kernel,
        out_shape=gradient_shapes(),
        in_specs=in_vmem(7),
        out_specs=in_vmem(3),
        scratch_shapes=[
            pltpu.VMEM((FRAMES, ROWS + 4, COLS, 3 * CH), BF),
            pltpu.VMEM((FRAMES, ROWS + 2, COLS, 3 * CH), BF),
        ],
        compiler_params=pltpu.CompilerParams(vmem_limit_bytes=24 << 20),
        name="two_blocks",
    )(low, own, high, w1, slope1, w0, slope0)


def tap_rows_kernel(act_ref, order_ref, out_ref, u_ref):
    for t in range(FRAMES):
        x = act_ref[t].reshape(-1, CH).astype(F32)
        u = (x * jax.nn.sigmoid(x)).astype(BF).astype(F32)
        col = lax.broadcasted_iota(jnp.int32, u.shape, 0) % COLS
        size = u.shape[0]
        before = jnp.where(col == 0, 0.0, pltpu.roll(u, 1, 0))
        after = jnp.where(col == COLS - 1, 0.0, pltpu.roll(u, size - 1, 0))
        for k, part in enumerate((before, u, after)):
            u_ref[k, t] = part.astype(BF).reshape(ROWS + 2, COLS, CH)
    for j in range(3):
        for k in range(3):
            taken = u_ref[k, :, j : j + ROWS].reshape(FRAMES * ROWS * COLS, CH)
            out_ref[3 * j + k] = lax.dot_general(
                order_ref[...], taken, (((1,), (1,)), ((), ())), preferred_element_type=F32
            ).astype(BF)


def tap_rows(act6, order):
    return pl.pallas_call(
        tap_rows_kernel,
        out_shape=jax.ShapeDtypeStruct((9, CH, FRAMES * ROWS * COLS), BF),
        in_specs=in_vmem(2),
        out_specs=pl.BlockSpec(memory_space=pltpu.VMEM),
        scratch_shapes=[pltpu.VMEM((3, FRAMES, ROWS + 2, COLS, CH), BF)],
        compiler_params=pltpu.CompilerParams(vmem_limit_bytes=24 << 20),
        name="tap_rows",
    )(act6, order)


def taps_kernel(scale, ut_ref, g_ref, out_ref):
    grad = g_ref[...].reshape(FRAMES, ROWS * COLS, CH)
    padded = jnp.concatenate([grad, jnp.zeros((2, ROWS * COLS, CH), BF)], axis=0)
    rhs = jnp.concatenate([padded[2 - i : 2 - i + FRAMES] for i in range(3)], axis=-1).reshape(
        FRAMES * ROWS * COLS, 3 * CH
    )
    for n in range(3):
        taps_here = slice(3 * n, 3 * n + 3)
        lhs = ut_ref[taps_here].reshape(3 * CH, FRAMES * ROWS * COLS)
        part = jnp.dot(lhs, rhs, preferred_element_type=F32)
        out_ref[taps_here] = (part * scale).astype(BF).reshape(3, CH, 3 * CH)


def taps(ut, grad, scale):
    return pl.pallas_call(
        functools.partial(taps_kernel, scale),
        out_shape=jax.ShapeDtypeStruct((9, CH, 3 * CH), BF),
        in_specs=in_vmem(2),
        out_specs=pl.BlockSpec(memory_space=pltpu.VMEM),
        compiler_params=pltpu.CompilerParams(vmem_limit_bytes=24 << 20),
        name="kernel_taps",
    )(ut, grad)


def channel_order():
    share = CH // DP
    order = []
    for n in range(CH):
        slot, rest = divmod(n, share)
        d = 0
        for place, bit in enumerate(HALVING):
            if (slot >> (len(HALVING) - 1 - place)) & 1:
                d |= bit
        order.append(d * share + rest)
    matrix = np.zeros((CH, CH), np.float32)
    matrix[np.arange(CH), order] = 1.0
    return matrix


def slope_of(x):
    x = x.astype(F32)
    sig = jax.nn.sigmoid(x)
    return sig * (1.0 + x * (1.0 - sig))


def as_matrix(kern):
    return jnp.transpose(kern, (1, 2, 4, 0, 3)).reshape(9 * CH, 3 * CH)


def local(acts, kernels, cotangent):
    me = lax.axis_index("section")
    dp = lax.axis_index("dp")
    core = dp % 2
    scale = 1.0 / math.sqrt(FRAMES * ROWS * DP * COLS)
    odd = [s for s in range(SEC) if s % 2 == 1]
    every = range(SEC)
    pair = odd[:-1]
    barrier = lax.optimization_barrier

    both = jnp.concatenate([cotangent, acts[0]], axis=0)
    edge_low = permute(both[:, -1:], [(s, s, 1) for s in every])
    edge_high = permute(both[:, :1], [(s, s, -1) for s in every])
    low0, high0 = edge_low[:FRAMES], edge_high[:FRAMES]
    act6 = jnp.concatenate([edge_low[FRAMES:], acts[0], edge_high[FRAMES:]], axis=1)

    w = as_matrix(kernels[0])
    half = w.shape[0] // 2
    w_half = permute(
        lax.dynamic_slice_in_dim(w, core * half, half, 0), [(s + 1, s, 0) for s in pair]
    )
    slope = slope_of(acts[0])
    none = jnp.zeros((FRAMES, 2, COLS, CH), BF)
    state = lax.cond(
        me == 7,
        lambda: tuple(single(low0, cotangent, high0, w, slope)),
        lambda: (cotangent, none, none),
    )

    act6, state = barrier((act6, state))
    act_next = permute(act6, [(s + 1, s, 0) for s in pair])
    w_other = lax.ppermute(
        w_half, AXES, [(s * DP + d, s * DP + (d ^ 1)) for s in pair for d in range(DP)]
    )
    w_next = jnp.where(
        core == 0,
        jnp.concatenate([w_half, w_other], axis=0),
        jnp.concatenate([w_other, w_half], axis=0),
    )
    row = lax.broadcasted_iota(jnp.int32, act_next.shape, 1) + dp * ROWS - 1
    inside = (row >= 0) & (row < DP * ROWS)
    slope_next = jnp.where(inside, slope_of(act_next), 0.0)

    def hop(state, target):
        result, top, bottom = state
        own = permute(result, [(target + 2, target, 0)])
        low = permute(bottom, [(target + 2, target, 1)])
        high = permute(top, [(target + 2, target, -1)])
        return low, own, high

    def stage(state, arrived, section):
        low, own, high = arrived
        return lax.cond(
            me == section,
            lambda: tuple(double(low, own, high, w_next, slope_next, w, slope)),
            lambda: state,
        )

    state = stage(state, hop(state, 5), 5)
    state = stage(state, hop(state, 3), 3)
    act6, state = barrier((act6, state))
    arrived = hop(state, 1)
    act_prev = permute(act6, [(s, (s + 1) % SEC, 0) for s in every])
    ut = tap_rows(act_prev, jnp.asarray(channel_order(), BF))
    ut, arrived = barrier((ut, arrived))
    result, _, _ = stage(state, arrived, 1)

    def even(result, sections):
        hops = [(s + 1, s) for s in sections]
        own = permute(result, [(a, b, 0) for a, b in hops])
        low = permute(result[:, -1:], [(a, b, 1) for a, b in hops])
        high = permute(result[:, :1], [(a, b, -1) for a, b in hops])
        live = functools.reduce(jnp.logical_or, [me == s for s in sections])
        return lax.cond(
            live,
            lambda: single(low, own, high, w, slope)[0],
            lambda: result,
        )

    result = even(result, (6, 4, 2))
    final = even(result, (0,))

    grad = jnp.where(me == 0, cotangent, result)
    part = taps(ut, grad, scale)
    for bit in HALVING:
        size = part.shape[1] // 2
        mine = (dp // bit) % 2
        keep = lax.dynamic_slice_in_dim(part, mine * size, size, 1)
        give = lax.dynamic_slice_in_dim(part, (1 - mine) * size, size, 1)
        shift = 0
        if bit == HALVING[-1]:
            keep = permute(keep, [((s + 1) % SEC, s, 0) for s in every])
            shift = 1
        got = lax.ppermute(
            give,
            AXES,
            [((s + shift) % SEC * DP + d, s * DP + (d ^ bit)) for s in every for d in range(DP)],
        )
        part = keep.astype(F32) + got.astype(F32)
        if not shift:
            part = part.astype(BF)
    share = CH // DP
    kernel_part = jnp.transpose(part.reshape(9, share, 3, CH), (1, 2, 0, 3)).reshape(share, 27, CH)
    return (final[None], kernel_part[None])


def solution(mesh):
    return jax.shard_map(
        local,
        mesh=mesh,
        in_specs=(
            P("section", None, "dp", None, None),
            P("section", None, None, None, None, None),
            P(None, "dp", None, None),
        ),
        out_specs=(P("section", None, "dp", None, None), P("section", "dp", None, None)),
        check_vma=False,
    )
```

```python
import functools
import math

import jax
import jax.numpy as jnp
import numpy as np
from jax import lax
from jax.experimental import pallas as pl
from jax.experimental.pallas import tpu as pltpu
from jax.sharding import PartitionSpec as P

BF = jnp.bfloat16
F32 = jnp.float32
DP = 32
SEC = 8
FRAMES = 9
ROWS = 4
COLS = 32
CH = 128
AXES = ("section", "dp")
HALVING = (1, 4, 2, 8, 16)


def permute(value, hops):
    pairs = [
        (src * DP + d, dst * DP + d + off)
        for src, dst, off in hops
        for d in range(DP)
        if 0 <= d + off < DP
    ]
    return lax.ppermute(value, AXES, pairs)


def fill(x_ref, frame, row, value):
    count = value.shape[0] // COLS
    col = lax.broadcasted_iota(jnp.int32, value.shape, 0) % COLS
    size = value.shape[0]
    after = jnp.where(col == COLS - 1, 0.0, pltpu.roll(value, size - 1, 0))
    before = jnp.where(col == 0, 0.0, pltpu.roll(value, 1, 0))
    for n, part in enumerate((after, value, before)):
        x_ref[frame, row : row + count, :, n * CH : (n + 1) * CH] = part.astype(BF).reshape(
            count, COLS, CH
        )


def back_pass(x_ref, w_ref, slope_ref, rows, emit):
    group = 3
    size = rows * COLS
    one_later = None
    two_later = None
    for start in range(FRAMES - group, -1, -group):
        lhs = jnp.concatenate(
            [x_ref[start : start + group, 2 - j : 2 - j + rows] for j in range(3)], axis=-1
        ).reshape(group * size, 9 * CH)
        part = jnp.dot(lhs, w_ref[...], preferred_element_type=F32)
        for t in range(group - 1, -1, -1):
            here = part[t * size : (t + 1) * size]
            back = here[:, 2 * CH :]
            if one_later is not None:
                back = back + one_later[:, CH : 2 * CH]
            if two_later is not None:
                back = back + two_later[:, :CH]
            frame = start + t
            grad = x_ref[frame, 1 : 1 + rows, :, CH : 2 * CH].reshape(size, CH).astype(F32)
            new = grad + slope_ref[frame].reshape(size, CH) * back
            emit(frame, new.astype(BF))
            two_later = one_later
            one_later = here


def emit_to(refs):
    out_ref, top_ref, bottom_ref = refs

    def emit(frame, value):
        whole = value.reshape(ROWS, COLS, CH)
        out_ref[frame] = whole
        top_ref[frame] = whole[:2]
        bottom_ref[frame] = whole[2:]

    return emit


def single_kernel(low_ref, own_ref, high_ref, w_ref, slope_ref, *rest):
    *outs, x_ref = rest
    for t in range(FRAMES):
        whole = jnp.concatenate([low_ref[t], own_ref[t], high_ref[t]], axis=0)
        fill(x_ref, t, 0, whole.reshape(-1, CH).astype(F32))
    back_pass(x_ref, w_ref, slope_ref, ROWS, emit_to(outs))


def double_kernel(low_ref, own_ref, high_ref, w1_ref, slope1_ref, w0_ref, slope0_ref, *rest):
    *outs, x1_ref, x0_ref = rest
    for t in range(FRAMES):
        whole = jnp.concatenate([low_ref[t], own_ref[t], high_ref[t]], axis=0)
        fill(x1_ref, t, 0, whole.reshape(-1, CH).astype(F32))

    def emit_mid(frame, value):
        fill(x0_ref, frame, 0, value.astype(F32))

    back_pass(x1_ref, w1_ref, slope1_ref, ROWS + 2, emit_mid)
    back_pass(x0_ref, w0_ref, slope0_ref, ROWS, emit_to(outs))


def in_vmem(count):
    return [pl.BlockSpec(memory_space=pltpu.VMEM)] * count


def gradient_shapes():
    return [
        jax.ShapeDtypeStruct((FRAMES, rows, COLS, CH), BF) for rows in (ROWS, 2, 2)
    ]


def single(low, own, high, w, slope):
    return pl.pallas_call(
        single_kernel,
        out_shape=gradient_shapes(),
        in_specs=in_vmem(5),
        out_specs=in_vmem(3),
        scratch_shapes=[pltpu.VMEM((FRAMES, ROWS + 2, COLS, 3 * CH), BF)],
        compiler_params=pltpu.CompilerParams(vmem_limit_bytes=24 << 20),
        name="one_block",
    )(low, own, high, w, slope)


def double(low, own, high, w1, slope1, w0, slope0):
    return pl.pallas_call(
        double_kernel,
        out_shape=gradient_shapes(),
        in_specs=in_vmem(7),
        out_specs=in_vmem(3),
        scratch_shapes=[
            pltpu.VMEM((FRAMES, ROWS + 4, COLS, 3 * CH), BF),
            pltpu.VMEM((FRAMES, ROWS + 2, COLS, 3 * CH), BF),
        ],
        compiler_params=pltpu.CompilerParams(vmem_limit_bytes=24 << 20),
        name="two_blocks",
    )(low, own, high, w1, slope1, w0, slope0)


def tap_rows_kernel(act_ref, order_ref, out_ref, u_ref):
    for t in range(FRAMES):
        x = act_ref[t].reshape(-1, CH).astype(F32)
        u = (x * jax.nn.sigmoid(x)).astype(BF).astype(F32)
        col = lax.broadcasted_iota(jnp.int32, u.shape, 0) % COLS
        size = u.shape[0]
        before = jnp.where(col == 0, 0.0, pltpu.roll(u, 1, 0))
        after = jnp.where(col == COLS - 1, 0.0, pltpu.roll(u, size - 1, 0))
        for k, part in enumerate((before, u, after)):
            u_ref[k, t] = part.astype(BF).reshape(ROWS + 2, COLS, CH)
    for j in range(3):
        for k in range(3):
            taken = u_ref[k, :, j : j + ROWS].reshape(FRAMES * ROWS * COLS, CH)
            out_ref[3 * j + k] = lax.dot_general(
                order_ref[...], taken, (((1,), (1,)), ((), ())), preferred_element_type=F32
            ).astype(BF)


def tap_rows(act6, order):
    return pl.pallas_call(
        tap_rows_kernel,
        out_shape=jax.ShapeDtypeStruct((9, CH, FRAMES * ROWS * COLS), BF),
        in_specs=in_vmem(2),
        out_specs=pl.BlockSpec(memory_space=pltpu.VMEM),
        scratch_shapes=[pltpu.VMEM((3, FRAMES, ROWS + 2, COLS, CH), BF)],
        compiler_params=pltpu.CompilerParams(vmem_limit_bytes=24 << 20),
        name="tap_rows",
    )(act6, order)


def taps_kernel(scale, ut_ref, g_ref, out_ref):
    grad = g_ref[...].reshape(FRAMES, ROWS * COLS, CH)
    padded = jnp.concatenate([grad, jnp.zeros((2, ROWS * COLS, CH), BF)], axis=0)
    rhs = jnp.concatenate([padded[2 - i : 2 - i + FRAMES] for i in range(3)], axis=-1).reshape(
        FRAMES * ROWS * COLS, 3 * CH
    )
    for n in range(3):
        taps_here = slice(3 * n, 3 * n + 3)
        lhs = ut_ref[taps_here].reshape(3 * CH, FRAMES * ROWS * COLS)
        part = jnp.dot(lhs, rhs, preferred_element_type=F32)
        out_ref[taps_here] = (part * scale).astype(BF).reshape(3, CH, 3 * CH)


def taps(ut, grad, scale):
    return pl.pallas_call(
        functools.partial(taps_kernel, scale),
        out_shape=jax.ShapeDtypeStruct((9, CH, 3 * CH), BF),
        in_specs=in_vmem(2),
        out_specs=pl.BlockSpec(memory_space=pltpu.VMEM),
        compiler_params=pltpu.CompilerParams(vmem_limit_bytes=24 << 20),
        name="kernel_taps",
    )(ut, grad)


def channel_order():
    share = CH // DP
    order = []
    for n in range(CH):
        slot, rest = divmod(n, share)
        d = 0
        for place, bit in enumerate(HALVING):
            if (slot >> (len(HALVING) - 1 - place)) & 1:
                d |= bit
        order.append(d * share + rest)
    matrix = np.zeros((CH, CH), np.float32)
    matrix[np.arange(CH), order] = 1.0
    return matrix


def slope_of(x):
    x = x.astype(F32)
    sig = jax.nn.sigmoid(x)
    return sig * (1.0 + x * (1.0 - sig))


def as_matrix(kern):
    return jnp.transpose(kern, (1, 2, 4, 0, 3)).reshape(9 * CH, 3 * CH)


def local(acts, kernels, cotangent):
    me = lax.axis_index("section")
    dp = lax.axis_index("dp")
    core = dp % 2
    scale = 1.0 / math.sqrt(FRAMES * ROWS * DP * COLS)
    odd = [s for s in range(SEC) if s % 2 == 1]
    every = range(SEC)
    pair = odd[:-1]
    barrier = lax.optimization_barrier

    both = jnp.concatenate([cotangent, acts[0]], axis=0)
    kern, last_row, first_row = barrier((kernels[0], both[:, -1:], both[:, :1]))
    edge_low = permute(last_row, [(s, s, 1) for s in every])
    edge_high = permute(first_row, [(s, s, -1) for s in every])
    low0, high0 = edge_low[:FRAMES], edge_high[:FRAMES]
    act6 = jnp.concatenate([edge_low[FRAMES:], acts[0], edge_high[FRAMES:]], axis=1)

    w = as_matrix(kern)
    half = w.shape[0] // 2
    w_half = permute(
        lax.dynamic_slice_in_dim(w, core * half, half, 0), [(s + 1, s, 0) for s in pair]
    )
    slope = slope_of(acts[0])
    none = jnp.zeros((FRAMES, 2, COLS, CH), BF)
    state = lax.cond(
        me == 7,
        lambda: tuple(single(low0, cotangent, high0, w, slope)),
        lambda: (cotangent, none, none),
    )

    act6, state = barrier((act6, state))
    act_next = permute(act6, [(s + 1, s, 0) for s in pair])

    def hop(state, target):
        result, top, bottom = state
        own = permute(result, [(target + 2, target, 0)])
        low = permute(bottom, [(target + 2, target, 1)])
        high = permute(top, [(target + 2, target, -1)])
        return low, own, high

    low, own, high = hop(state, 5)
    w_half, low = barrier((w_half, low))
    w_other = lax.ppermute(
        w_half, AXES, [(s * DP + d, s * DP + (d ^ 1)) for s in pair for d in range(DP)]
    )
    w_next = jnp.where(
        core == 0,
        jnp.concatenate([w_half, w_other], axis=0),
        jnp.concatenate([w_other, w_half], axis=0),
    )
    row = lax.broadcasted_iota(jnp.int32, act_next.shape, 1) + dp * ROWS - 1
    inside = (row >= 0) & (row < DP * ROWS)
    slope_next = jnp.where(inside, slope_of(act_next), 0.0)

    def stage(state, arrived, section):
        low, own, high = arrived
        return lax.cond(
            me == section,
            lambda: tuple(double(low, own, high, w_next, slope_next, w, slope)),
            lambda: state,
        )

    state = stage(state, (low, own, high), 5)
    state = stage(state, hop(state, 3), 3)
    act6, state = barrier((act6, state))
    arrived = hop(state, 1)
    act_prev = permute(act6, [(s, (s + 1) % SEC, 0) for s in every])
    ut = tap_rows(act_prev, jnp.asarray(channel_order(), BF))
    ut, arrived = barrier((ut, arrived))
    result, _, _ = stage(state, arrived, 1)

    def even(result, sections):
        hops = [(s + 1, s) for s in sections]
        own = permute(result, [(a, b, 0) for a, b in hops])
        low = permute(result[:, -1:], [(a, b, 1) for a, b in hops])
        high = permute(result[:, :1], [(a, b, -1) for a, b in hops])
        live = functools.reduce(jnp.logical_or, [me == s for s in sections])
        return lax.cond(
            live,
            lambda: single(low, own, high, w, slope)[0],
            lambda: result,
        )

    grad = jnp.where(me == 0, cotangent, result)
    first = (me % 2 == 1) | (me == 0)
    part = lax.cond(
        first,
        lambda: taps(ut, grad, scale),
        lambda: jnp.zeros((9, CH, 3 * CH), BF),
    )
    result, part = barrier((result, part))
    result = even(result, (6, 4, 2))
    final = even(result, (0,))
    part = lax.cond(first, lambda: part, lambda: taps(ut, result, scale))
    for bit in HALVING[:3]:
        size = part.shape[1] // 2
        mine = (dp // bit) % 2
        keep = lax.dynamic_slice_in_dim(part, mine * size, size, 1)
        give = lax.dynamic_slice_in_dim(part, (1 - mine) * size, size, 1)
        got = lax.ppermute(
            give, AXES, [(s * DP + d, s * DP + (d ^ bit)) for s in every for d in range(DP)]
        )
        part = (keep.astype(F32) + got.astype(F32)).astype(BF)
    high_bit, low_bit = HALVING[3:]
    total = 0.0
    for a, b in ((1, 1), (0, 1), (1, 0), (0, 0)):
        flip = a * high_bit + b * low_bit
        slot = ((dp // high_bit + a) % 2) * 2 + (dp // low_bit + b) % 2
        piece = lax.dynamic_slice_in_dim(part, slot * (CH // DP), CH // DP, 1)
        pairs = [
            ((s + 1) % SEC * DP + d, s * DP + (d ^ flip)) for s in every for d in range(DP)
        ]
        total = total + lax.ppermute(piece, AXES, pairs).astype(F32)
    part = total
    share = CH // DP
    kernel_part = jnp.transpose(part.reshape(9, share, 3, CH), (1, 2, 0, 3)).reshape(share, 27, CH)
    return (final[None], kernel_part[None])


def solution(mesh):
    return jax.shard_map(
        local,
        mesh=mesh,
        in_specs=(
            P("section", None, "dp", None, None),
            P("section", None, None, None, None, None),
            P(None, "dp", None, None),
        ),
        out_specs=(P("section", None, "dp", None, None), P("section", "dp", None, None)),
        check_vma=False,
    )
```

```python
import functools
import math

import jax
import jax.numpy as jnp
import numpy as np
from jax import lax
from jax.experimental import pallas as pl
from jax.experimental.pallas import tpu as pltpu
from jax.sharding import PartitionSpec as P

BF = jnp.bfloat16
F32 = jnp.float32
DP = 32
SEC = 8
FRAMES = 9
ROWS = 4
COLS = 32
CH = 128
AXES = ("section", "dp")
HALVING = (1, 4, 2, 8, 16)


def permute(value, hops):
    pairs = [
        (src * DP + d, dst * DP + d + off)
        for src, dst, off in hops
        for d in range(DP)
        if 0 <= d + off < DP
    ]
    return lax.ppermute(value, AXES, pairs)


def fill(x_ref, frame, row, value):
    count = value.shape[0] // COLS
    col = lax.broadcasted_iota(jnp.int32, value.shape, 0) % COLS
    size = value.shape[0]
    after = jnp.where(col == COLS - 1, 0.0, pltpu.roll(value, size - 1, 0))
    before = jnp.where(col == 0, 0.0, pltpu.roll(value, 1, 0))
    for n, part in enumerate((after, value, before)):
        x_ref[frame, row : row + count, :, n * CH : (n + 1) * CH] = part.astype(BF).reshape(
            count, COLS, CH
        )


def weights(w_ref):
    return jnp.concatenate(
        [
            jnp.concatenate(
                [w_ref[(9 * i + n) * CH : (9 * i + n + 1) * CH, :] for n in range(9)], axis=1
            )
            for i in range(3)
        ],
        axis=0,
    )


def back_pass(x_ref, rhs, slope_ref, rows, emit):
    group = 3
    size = rows * COLS
    one_later = None
    two_later = None
    for start in range(FRAMES - group, -1, -group):
        lhs = jnp.concatenate(
            [x_ref[start : start + group, 2 - j : 2 - j + rows] for j in range(3)], axis=-1
        ).reshape(group * size, 9 * CH)
        part = lax.dot_general(
            lhs, rhs, (((1,), (1,)), ((), ())), preferred_element_type=F32
        )
        for t in range(group - 1, -1, -1):
            here = part[t * size : (t + 1) * size]
            back = here[:, 2 * CH :]
            if one_later is not None:
                back = back + one_later[:, CH : 2 * CH]
            if two_later is not None:
                back = back + two_later[:, :CH]
            frame = start + t
            grad = x_ref[frame, 1 : 1 + rows, :, CH : 2 * CH].reshape(size, CH).astype(F32)
            new = grad + slope_ref[frame].reshape(size, CH) * back
            emit(frame, new.astype(BF))
            two_later = one_later
            one_later = here


def emit_to(refs):
    out_ref, top_ref, bottom_ref = refs

    def emit(frame, value):
        whole = value.reshape(ROWS, COLS, CH)
        out_ref[frame] = whole
        top_ref[frame] = whole[:2]
        bottom_ref[frame] = whole[2:]

    return emit


def single_kernel(low_ref, own_ref, high_ref, w_ref, slope_ref, *rest):
    *outs, x_ref = rest
    for t in range(FRAMES):
        whole = jnp.concatenate([low_ref[t], own_ref[t], high_ref[t]], axis=0)
        fill(x_ref, t, 0, whole.reshape(-1, CH).astype(F32))
    back_pass(x_ref, weights(w_ref), slope_ref, ROWS, emit_to(outs))


def double_kernel(
    core_ref, low_ref, own_ref, high_ref, half_ref, other_ref, slope1_ref, w0_ref, slope0_ref, *rest
):
    *outs, x1_ref, x0_ref, w1_ref = rest
    half = half_ref.shape[0]
    core = core_ref[0]
    w1_ref[pl.ds(pl.multiple_of(core * half, half), half), :] = half_ref[...]
    w1_ref[pl.ds(pl.multiple_of((1 - core) * half, half), half), :] = other_ref[...]
    for t in range(FRAMES):
        whole = jnp.concatenate([low_ref[t], own_ref[t], high_ref[t]], axis=0)
        fill(x1_ref, t, 0, whole.reshape(-1, CH).astype(F32))

    def emit_mid(frame, value):
        fill(x0_ref, frame, 0, value.astype(F32))

    back_pass(x1_ref, weights(w1_ref), slope1_ref, ROWS + 2, emit_mid)
    back_pass(x0_ref, weights(w0_ref), slope0_ref, ROWS, emit_to(outs))


def in_vmem(count):
    return [pl.BlockSpec(memory_space=pltpu.VMEM)] * count


def gradient_shapes():
    return [
        jax.ShapeDtypeStruct((FRAMES, rows, COLS, CH), BF) for rows in (ROWS, 2, 2)
    ]


def single(low, own, high, w, slope):
    return pl.pallas_call(
        single_kernel,
        out_shape=gradient_shapes(),
        in_specs=in_vmem(5),
        out_specs=in_vmem(3),
        scratch_shapes=[pltpu.VMEM((FRAMES, ROWS + 2, COLS, 3 * CH), BF)],
        compiler_params=pltpu.CompilerParams(vmem_limit_bytes=24 << 20),
        name="one_block",
    )(low, own, high, w, slope)


def double(core, low, own, high, half, other, slope1, w0, slope0):
    return pl.pallas_call(
        double_kernel,
        out_shape=gradient_shapes(),
        in_specs=[pl.BlockSpec(memory_space=pltpu.SMEM)] + in_vmem(8),
        out_specs=in_vmem(3),
        scratch_shapes=[
            pltpu.VMEM((FRAMES, ROWS + 4, COLS, 3 * CH), BF),
            pltpu.VMEM((FRAMES, ROWS + 2, COLS, 3 * CH), BF),
            pltpu.VMEM((27 * CH, CH), BF),
        ],
        compiler_params=pltpu.CompilerParams(vmem_limit_bytes=24 << 20),
        name="two_blocks",
    )(core.reshape(1), low, own, high, half, other, slope1, w0, slope0)


def tap_rows_kernel(act_ref, order_ref, out_ref, u_ref):
    for t in range(FRAMES):
        x = act_ref[t].reshape(-1, CH).astype(F32)
        u = (x * jax.nn.sigmoid(x)).astype(BF).astype(F32)
        col = lax.broadcasted_iota(jnp.int32, u.shape, 0) % COLS
        size = u.shape[0]
        before = jnp.where(col == 0, 0.0, pltpu.roll(u, 1, 0))
        after = jnp.where(col == COLS - 1, 0.0, pltpu.roll(u, size - 1, 0))
        for k, part in enumerate((before, u, after)):
            u_ref[k, t] = part.astype(BF).reshape(ROWS + 2, COLS, CH)
    for j in range(3):
        for k in range(3):
            taken = u_ref[k, :, j : j + ROWS].reshape(FRAMES * ROWS * COLS, CH)
            out_ref[3 * j + k] = lax.dot_general(
                order_ref[...], taken, (((1,), (1,)), ((), ())), preferred_element_type=F32
            ).astype(BF)


def tap_rows(act6, order):
    return pl.pallas_call(
        tap_rows_kernel,
        out_shape=jax.ShapeDtypeStruct((9, CH, FRAMES * ROWS * COLS), BF),
        in_specs=in_vmem(2),
        out_specs=pl.BlockSpec(memory_space=pltpu.VMEM),
        scratch_shapes=[pltpu.VMEM((3, FRAMES, ROWS + 2, COLS, CH), BF)],
        compiler_params=pltpu.CompilerParams(vmem_limit_bytes=24 << 20),
        name="tap_rows",
    )(act6, order)


def taps_kernel(scale, ut_ref, g_ref, out_ref):
    grad = g_ref[...].reshape(FRAMES, ROWS * COLS, CH)
    padded = jnp.concatenate([grad, jnp.zeros((2, ROWS * COLS, CH), BF)], axis=0)
    rhs = jnp.concatenate([padded[2 - i : 2 - i + FRAMES] for i in range(3)], axis=-1).reshape(
        FRAMES * ROWS * COLS, 3 * CH
    )
    for n in range(3):
        taps_here = slice(3 * n, 3 * n + 3)
        lhs = ut_ref[taps_here].reshape(3 * CH, FRAMES * ROWS * COLS)
        part = jnp.dot(lhs, rhs, preferred_element_type=F32)
        out_ref[taps_here] = (part * scale).astype(BF).reshape(3, CH, 3 * CH)


def taps(ut, grad, scale):
    return pl.pallas_call(
        functools.partial(taps_kernel, scale),
        out_shape=jax.ShapeDtypeStruct((9, CH, 3 * CH), BF),
        in_specs=in_vmem(2),
        out_specs=pl.BlockSpec(memory_space=pltpu.VMEM),
        compiler_params=pltpu.CompilerParams(vmem_limit_bytes=24 << 20),
        name="kernel_taps",
    )(ut, grad)


def channel_order():
    share = CH // DP
    order = []
    for n in range(CH):
        slot, rest = divmod(n, share)
        d = 0
        for place, bit in enumerate(HALVING):
            if (slot >> (len(HALVING) - 1 - place)) & 1:
                d |= bit
        order.append(d * share + rest)
    matrix = np.zeros((CH, CH), np.float32)
    matrix[np.arange(CH), order] = 1.0
    return matrix


def slope_of(x):
    x = x.astype(F32)
    sig = jax.nn.sigmoid(x)
    return sig * (1.0 + x * (1.0 - sig))


def local(acts, kernels, cotangent):
    me = lax.axis_index("section")
    dp = lax.axis_index("dp")
    core = dp % 2
    scale = 1.0 / math.sqrt(FRAMES * ROWS * DP * COLS)
    odd = [s for s in range(SEC) if s % 2 == 1]
    every = range(SEC)
    pair = odd[:-1]
    barrier = lax.optimization_barrier

    w = kernels[0].reshape(27 * CH, CH)
    half = w.shape[0] // 2
    w_half = permute(
        lax.dynamic_slice_in_dim(w, core * half, half, 0), [(s + 1, s, 0) for s in pair]
    )

    both = jnp.concatenate([cotangent, acts[0]], axis=0)
    edge_low = permute(both[:, -1:], [(s, s, 1) for s in every])
    edge_high = permute(both[:, :1], [(s, s, -1) for s in every])
    low0, high0 = edge_low[:FRAMES], edge_high[:FRAMES]
    act6 = jnp.concatenate([edge_low[FRAMES:], acts[0], edge_high[FRAMES:]], axis=1)

    slope = slope_of(acts[0])
    none = jnp.zeros((FRAMES, 2, COLS, CH), BF)
    state = lax.cond(
        me == 7,
        lambda: tuple(single(low0, cotangent, high0, w, slope)),
        lambda: (cotangent, none, none),
    )

    def hop(state, target):
        result, top, bottom = state
        own = permute(result, [(target + 2, target, 0)])
        low = permute(bottom, [(target + 2, target, 1)])
        high = permute(top, [(target + 2, target, -1)])
        return low, own, high

    act6, state = barrier((act6, state))
    act_next = permute(act6, [(s + 1, s, 0) for s in pair])
    arrived, w_half = barrier((hop(state, 5), w_half))
    w_other = lax.ppermute(
        w_half, AXES, [(s * DP + d, s * DP + (d ^ 1)) for s in pair for d in range(DP)]
    )
    row = lax.broadcasted_iota(jnp.int32, act_next.shape, 1) + dp * ROWS - 1
    inside = (row >= 0) & (row < DP * ROWS)
    slope_next = jnp.where(inside, slope_of(act_next), 0.0)

    def stage(state, arrived, section):
        low, own, high = arrived
        return lax.cond(
            me == section,
            lambda: tuple(
                double(core, low, own, high, w_half, w_other, slope_next, w, slope)
            ),
            lambda: state,
        )

    def even(result, sections):
        hops = [(s + 1, s) for s in sections]
        own = permute(result, [(a, b, 0) for a, b in hops])
        low = permute(result[:, -1:], [(a, b, 1) for a, b in hops])
        high = permute(result[:, :1], [(a, b, -1) for a, b in hops])
        live = functools.reduce(jnp.logical_or, [me == s for s in sections])
        return lax.cond(
            live,
            lambda: single(low, own, high, w, slope)[0],
            lambda: result,
        )

    state = stage(state, arrived, 5)
    act6, state = barrier((act6, state))
    arrived = hop(state, 3)
    act_prev = permute(act6, [(s, (s + 1) % SEC, 0) for s in every])
    ut = tap_rows(act_prev, jnp.asarray(channel_order(), BF))
    ut, arrived = barrier((ut, arrived))
    state = stage(state, arrived, 3)
    arrived = hop(state, 1)
    result = even(state[0], (6, 4, 2))
    result, arrived = barrier((result, arrived))
    result, _, _ = stage((result, state[1], state[2]), arrived, 1)
    final = even(result, (0,))

    part = taps(ut, jnp.where(me == 0, cotangent, result), scale)
    for bit in HALVING:
        size = part.shape[1] // 2
        mine = (dp // bit) % 2
        keep = lax.dynamic_slice_in_dim(part, mine * size, size, 1)
        give = lax.dynamic_slice_in_dim(part, (1 - mine) * size, size, 1)
        shift = 0
        if bit == HALVING[-1]:
            keep = permute(keep, [((s + 1) % SEC, s, 0) for s in every])
            shift = 1
        got = lax.ppermute(
            give,
            AXES,
            [((s + shift) % SEC * DP + d, s * DP + (d ^ bit)) for s in every for d in range(DP)],
        )
        part = keep.astype(F32) + got.astype(F32)
        if not shift:
            part = part.astype(BF)
    share = CH // DP
    kernel_part = jnp.transpose(part.reshape(9, share, 3, CH), (1, 2, 0, 3)).reshape(share, 27, CH)
    return (final[None], kernel_part[None])


def solution(mesh):
    return jax.shard_map(
        local,
        mesh=mesh,
        in_specs=(
            P("section", None, "dp", None, None),
            P("section", None, None, None, None, None),
            P(None, "dp", None, None),
        ),
        out_specs=(P("section", None, "dp", None, None), P("section", "dp", None, None)),
        check_vma=False,
    )
```

```python
import functools
import math

import jax
import jax.numpy as jnp
import numpy as np
from jax import lax
from jax.experimental import pallas as pl
from jax.experimental.pallas import tpu as pltpu
from jax.sharding import PartitionSpec as P

BF = jnp.bfloat16
F32 = jnp.float32
DP = 32
SEC = 8
FRAMES = 9
CUT = 4
ROWS = 4
COLS = 32
CH = 128
AXES = ("section", "dp")
HALVING = (1, 2, 4, 8, 16)


def permute(value, hops):
    pairs = [
        (src * DP + d, dst * DP + d + off)
        for src, dst, off in hops
        for d in range(DP)
        if 0 <= d + off < DP
    ]
    return lax.ppermute(value, AXES, pairs)


def fill(x_ref, frame, row, value):
    count = value.shape[0] // COLS
    col = lax.broadcasted_iota(jnp.int32, value.shape, 0) % COLS
    size = value.shape[0]
    after = jnp.where(col == COLS - 1, 0.0, pltpu.roll(value, size - 1, 0))
    before = jnp.where(col == 0, 0.0, pltpu.roll(value, 1, 0))
    for n, part in enumerate((after, value, before)):
        x_ref[frame, row : row + count, :, n * CH : (n + 1) * CH] = part.astype(BF).reshape(
            count, COLS, CH
        )


def weights(w_ref):
    return jnp.concatenate(
        [
            jnp.concatenate(
                [w_ref[(9 * i + n) * CH : (9 * i + n + 1) * CH, :] for n in range(9)], axis=1
            )
            for i in range(3)
        ],
        axis=0,
    )


def back_pass(x_ref, rhs, slope_ref, rows, first, emit, carry_in=None, carry_out=None):
    size = rows * COLS
    count = x_ref.shape[0]
    group = count if count <= 5 else 3
    middle = lower = next_lower = None
    if carry_in is not None:
        middle, lower, next_lower = (
            carry_in[:, n * CH : (n + 1) * CH] for n in range(3)
        )
    for start in range(count - group, -1, -group):
        lhs = jnp.concatenate(
            [x_ref[start : start + group, 2 - j : 2 - j + rows] for j in range(3)], axis=-1
        ).reshape(group * size, 9 * CH)
        part = lax.dot_general(
            lhs, rhs, (((1,), (1,)), ((), ())), preferred_element_type=F32
        )
        for t in range(group - 1, -1, -1):
            here = part[t * size : (t + 1) * size]
            back = here[:, 2 * CH :]
            if middle is not None:
                back = back + middle
            if lower is not None:
                back = back + lower
            frame = start + t
            grad = x_ref[frame, 1 : 1 + rows, :, CH : 2 * CH].reshape(size, CH).astype(F32)
            new = grad + slope_ref[first + frame].reshape(size, CH) * back
            emit(frame, new.astype(BF))
            lower = next_lower
            next_lower = here[:, :CH]
            middle = here[:, CH : 2 * CH]
    if carry_out is not None:
        for n, value in enumerate((middle, lower, next_lower)):
            carry_out[:, n * CH : (n + 1) * CH] = value


def load(low_ref, own_ref, high_ref, x_ref):
    for t in range(own_ref.shape[0]):
        whole = jnp.concatenate([low_ref[t], own_ref[t], high_ref[t]], axis=0)
        fill(x_ref, t, 0, whole.reshape(-1, CH).astype(F32))


def emit_to(refs):
    out_ref, top_ref, bottom_ref = refs

    def emit(frame, value):
        whole = value.reshape(ROWS, COLS, CH)
        out_ref[frame] = whole
        top_ref[frame] = whole[:2]
        bottom_ref[frame] = whole[2:]

    return emit


def single_kernel(first, last, low_ref, own_ref, high_ref, w_ref, slope_ref, *rest):
    *outs, x_ref = rest
    load(low_ref, own_ref, high_ref, x_ref)
    back_pass(x_ref, weights(w_ref), slope_ref, ROWS, first, emit_to(outs))


def keep(flags_ref, previous, outs):
    @pl.when(flags_ref[0] == 0)
    def _():
        for source, target in zip(previous, outs, strict=True):
            target[...] = source[...]


def first_kernel(first, flags_ref, low_ref, own_ref, high_ref, w_ref, slope_ref, *rest):
    carry_in = carry_out = None
    if first == 0:
        carry_in, *rest = rest
    *outs, x_ref = rest[3:]
    if first > 0:
        *outs, carry_out = outs
    keep(flags_ref, rest[:3], outs)

    @pl.when(flags_ref[0] == 1)
    def _():
        load(low_ref, own_ref, high_ref, x_ref)
        back_pass(
            x_ref, weights(w_ref), slope_ref, ROWS, first, emit_to(outs), carry_in, carry_out
        )


def double_kernel(
    first,
    flags_ref,
    low_ref,
    own_ref,
    high_ref,
    half_ref,
    other_ref,
    slope1_ref,
    w0_ref,
    slope0_ref,
    *rest,
):
    in1 = in0 = out1 = out0 = None
    if first == 0:
        in1, in0, *rest = rest
    *outs, x1_ref, x0_ref, w1_ref = rest[3:]
    if first > 0:
        *outs, out1, out0 = outs
    keep(flags_ref, rest[:3], outs)

    def emit_mid(frame, value):
        fill(x0_ref, frame, 0, value.astype(F32))

    @pl.when(flags_ref[0] == 1)
    def _():
        half = half_ref.shape[0]
        core = flags_ref[1]
        w1_ref[pl.ds(pl.multiple_of(core * half, half), half), :] = half_ref[...]
        w1_ref[pl.ds(pl.multiple_of((1 - core) * half, half), half), :] = other_ref[...]
        load(low_ref, own_ref, high_ref, x1_ref)
        back_pass(x1_ref, weights(w1_ref), slope1_ref, ROWS + 2, first, emit_mid, in1, out1)
        back_pass(x0_ref, weights(w0_ref), slope0_ref, ROWS, first, emit_to(outs), in0, out0)


def in_vmem(count):
    return [pl.BlockSpec(memory_space=pltpu.VMEM)] * count


def gradient_shapes(count):
    return [jax.ShapeDtypeStruct((count, rows, COLS, CH), BF) for rows in (ROWS, 2, 2)]


def work(rows):
    positions = rows * COLS
    return pl.CostEstimate(
        flops=2 * positions * 27 * CH * CH * 3,
        bytes_accessed=positions * CH * 8 + 27 * CH * CH * 2,
        transcendentals=0,
    )


def carry_shape(rows):
    return jax.ShapeDtypeStruct((rows * COLS, 3 * CH), F32)


def single(low, own, high, w, slope):
    return pl.pallas_call(
        functools.partial(single_kernel, 0, FRAMES),
        out_shape=gradient_shapes(FRAMES),
        in_specs=in_vmem(5),
        out_specs=in_vmem(3),
        scratch_shapes=[pltpu.VMEM((FRAMES, ROWS + 2, COLS, 3 * CH), BF)],
        compiler_params=pltpu.CompilerParams(vmem_limit_bytes=24 << 20),
        cost_estimate=work(FRAMES * ROWS),
        name="one_block",
    )(low, own, high, w, slope)


def chain_call(kernel, name, first, last, live, core, operands, carry, previous, carries, rows):
    count = last - first
    out_shape = gradient_shapes(count)
    if first:
        out_shape += [carry_shape(r) for r in carries]
    scratch = [
        pltpu.VMEM((count, r + 2, COLS, 3 * CH), BF) for r in rows
    ]
    if len(rows) > 1:
        scratch.append(pltpu.VMEM((27 * CH, CH), BF))
    before = 1 + len(operands) + len(carry)
    flags = jnp.stack([live.astype(jnp.int32), core.astype(jnp.int32)])
    return pl.pallas_call(
        functools.partial(kernel, first),
        out_shape=out_shape,
        in_specs=[pl.BlockSpec(memory_space=pltpu.SMEM)] + in_vmem(before - 1 + 3),
        out_specs=in_vmem(len(out_shape)),
        scratch_shapes=scratch,
        input_output_aliases={before + n: n for n in range(3)},
        compiler_params=pltpu.CompilerParams(vmem_limit_bytes=24 << 20),
        cost_estimate=work(count * sum(rows)),
        name=f"{name}_{first}_{last}",
    )(flags, *operands, *carry, *previous)


def tap_rows_kernel(act_ref, order_ref, out_ref, u_ref):
    for t in range(FRAMES):
        x = act_ref[t].reshape(-1, CH).astype(F32)
        u = (x * jax.nn.sigmoid(x)).astype(BF).astype(F32)
        col = lax.broadcasted_iota(jnp.int32, u.shape, 0) % COLS
        size = u.shape[0]
        before = jnp.where(col == 0, 0.0, pltpu.roll(u, 1, 0))
        after = jnp.where(col == COLS - 1, 0.0, pltpu.roll(u, size - 1, 0))
        for k, part in enumerate((before, u, after)):
            u_ref[k, t] = part.astype(BF).reshape(ROWS + 2, COLS, CH)
    for j in range(3):
        for k in range(3):
            taken = u_ref[k, :, j : j + ROWS].reshape(FRAMES * ROWS * COLS, CH)
            out_ref[3 * j + k] = lax.dot_general(
                order_ref[...], taken, (((1,), (1,)), ((), ())), preferred_element_type=F32
            ).astype(BF)


def tap_rows(act6, order):
    return pl.pallas_call(
        tap_rows_kernel,
        out_shape=jax.ShapeDtypeStruct((9, CH, FRAMES * ROWS * COLS), BF),
        in_specs=in_vmem(2),
        out_specs=pl.BlockSpec(memory_space=pltpu.VMEM),
        scratch_shapes=[pltpu.VMEM((3, FRAMES, ROWS + 2, COLS, CH), BF)],
        compiler_params=pltpu.CompilerParams(vmem_limit_bytes=24 << 20),
        name="tap_rows",
    )(act6, order)


def taps_kernel(scale, ut_ref, early_ref, late_ref, out_ref):
    grad = jnp.concatenate([early_ref[...], late_ref[...]], axis=0).reshape(
        FRAMES, ROWS * COLS, CH
    )
    padded = jnp.concatenate([grad, jnp.zeros((2, ROWS * COLS, CH), BF)], axis=0)
    rhs = jnp.concatenate([padded[2 - i : 2 - i + FRAMES] for i in range(3)], axis=-1).reshape(
        FRAMES * ROWS * COLS, 3 * CH
    )
    for n in range(3):
        taps_here = slice(3 * n, 3 * n + 3)
        lhs = ut_ref[taps_here].reshape(3 * CH, FRAMES * ROWS * COLS)
        part = jnp.dot(lhs, rhs, preferred_element_type=F32)
        out_ref[taps_here] = (part * scale).astype(BF).reshape(3, CH, 3 * CH)


def taps(ut, early, late, scale):
    return pl.pallas_call(
        functools.partial(taps_kernel, scale),
        out_shape=jax.ShapeDtypeStruct((9, CH, 3 * CH), BF),
        in_specs=in_vmem(3),
        out_specs=pl.BlockSpec(memory_space=pltpu.VMEM),
        compiler_params=pltpu.CompilerParams(vmem_limit_bytes=24 << 20),
        name="kernel_taps",
    )(ut, early, late)


def channel_order():
    share = CH // DP
    order = []
    for n in range(CH):
        slot, rest = divmod(n, share)
        d = 0
        for place, bit in enumerate(HALVING):
            if (slot >> (len(HALVING) - 1 - place)) & 1:
                d |= bit
        order.append(d * share + rest)
    matrix = np.zeros((CH, CH), np.float32)
    matrix[np.arange(CH), order] = 1.0
    return matrix


def slope_of(x):
    x = x.astype(F32)
    sig = jax.nn.sigmoid(x)
    return sig * (1.0 + x * (1.0 - sig))


def local(acts, kernels, cotangent):
    me = lax.axis_index("section")
    dp = lax.axis_index("dp")
    core = dp % 2
    scale = 1.0 / math.sqrt(FRAMES * ROWS * DP * COLS)
    odd = [s for s in range(SEC) if s % 2 == 1]
    every = range(SEC)
    pair = odd[:-1]
    barrier = lax.optimization_barrier

    w = kernels[0].reshape(27 * CH, CH)
    half = w.shape[0] // 2
    w_half = permute(
        lax.dynamic_slice_in_dim(w, core * half, half, 0), [(s + 1, s, 0) for s in pair]
    )

    both = jnp.concatenate([cotangent, acts[0]], axis=0)
    edge_low = permute(both[:, -1:], [(s, s, 1) for s in every])
    edge_high = permute(both[:, :1], [(s, s, -1) for s in every])
    low0, high0 = edge_low[:FRAMES], edge_high[:FRAMES]
    act6 = jnp.concatenate([edge_low[FRAMES:], acts[0], edge_high[FRAMES:]], axis=1)

    slope = slope_of(acts[0])
    chunks = {"late": (CUT, FRAMES), "early": (0, CUT)}

    def blank(count):
        return tuple(jnp.zeros((count, 2, COLS, CH), BF) for _ in range(2))

    def start_stage(name, carry):
        first, last = chunks[name]
        part = slice(first, last)
        return chain_call(
            first_kernel,
            "first_block",
            first,
            last,
            me == 7,
            core,
            (low0[part], cotangent[part], high0[part], w, slope),
            carry,
            (cotangent[part],) + blank(last - first),
            (ROWS,),
            (ROWS,),
        )

    def hop(state, target):
        result, top, bottom = state[:3]
        own = permute(result, [(target + 2, target, 0)])
        low = permute(bottom, [(target + 2, target, 1)])
        high = permute(top, [(target + 2, target, -1)])
        return low, own, high

    late7 = start_stage("late", ())
    act6, w_half = barrier((act6, w_half))
    act_next = permute(act6, [(s + 1, s, 0) for s in pair])
    w_other = lax.ppermute(
        w_half, AXES, [(s * DP + d, s * DP + (d ^ 1)) for s in pair for d in range(DP)]
    )
    row = lax.broadcasted_iota(jnp.int32, act_next.shape, 1) + dp * ROWS - 1
    inside = (row >= 0) & (row < DP * ROWS)
    slope_next = jnp.where(inside, slope_of(act_next), 0.0)

    def pair_stage(name, section, previous, arrived, carry):
        first, last = chunks[name]
        return chain_call(
            double_kernel,
            "two_blocks",
            first,
            last,
            me == section,
            core,
            (*arrived, w_half, w_other, slope_next, w, slope),
            carry,
            tuple(previous[:3]),
            (ROWS + 2, ROWS),
            (ROWS + 2, ROWS),
        )

    def even(early, late, sections):
        hops = [(s + 1, s) for s in sections]
        own, top, bottom = (
            jnp.concatenate([a, b], axis=0) for a, b in zip(early[:3], late[:3], strict=True)
        )
        own = permute(own, [(a, b, 0) for a, b in hops])
        low = permute(bottom[:, 1:], [(a, b, 1) for a, b in hops])
        high = permute(top[:, :1], [(a, b, -1) for a, b in hops])
        live = functools.reduce(jnp.logical_or, [me == s for s in sections])

        def run():
            new = single(low, own, high, w, slope)[0]
            return new[:CUT], new[CUT:]

        return lax.cond(live, run, lambda: (early[0], late[0]))

    late_in = hop(late7, 5)
    late5 = pair_stage("late", 5, late7, late_in, ())
    carry, late5 = barrier((late7[3:], late5))
    early7 = start_stage("early", carry)
    early_in = hop(early7, 5)

    late_in = hop(late5, 3)
    act_prev = permute(act6, [(s, (s + 1) % SEC, 0) for s in every])
    ut = tap_rows(act_prev, jnp.asarray(channel_order(), BF))
    ut, late_in = barrier((ut, late_in))
    late3 = pair_stage("late", 3, late5, late_in, ())
    carry, late3 = barrier((late5[3:], late3))
    early5 = pair_stage("early", 5, early7, early_in, carry)
    early_in = hop(early5, 3)

    late_in = hop(late3, 1)
    late1 = pair_stage("late", 1, late3, late_in, ())
    carry, late1 = barrier((late3[3:], late1))
    early3 = pair_stage("early", 3, early5, early_in, carry)
    early_in = hop(early3, 1)

    early_even, late_even = even(early3, late3, (6, 4, 2))
    early_even, early_in = barrier((early_even, early_in))
    early1 = pair_stage("early", 1, early3, early_in, late1[3:])

    early = lax.select(me % 2 == 1, early1[0], early_even)
    late = lax.select(me % 2 == 1, late1[0], late_even)
    is_first = me == 0
    part = taps(
        ut,
        jnp.where(is_first, cotangent[:CUT], early),
        jnp.where(is_first, cotangent[CUT:], late),
        scale,
    )
    early, late = even((early, *early1[1:3]), (late, *late1[1:3]), (0,))
    final = jnp.concatenate([early, late], axis=0)
    for bit in HALVING:
        size = part.shape[1] // 2
        mine = (dp // bit) % 2
        keep = lax.dynamic_slice_in_dim(part, mine * size, size, 1)
        give = lax.dynamic_slice_in_dim(part, (1 - mine) * size, size, 1)
        shift = 0
        if bit == HALVING[-1]:
            keep = permute(keep, [((s + 1) % SEC, s, 0) for s in every])
            shift = 1
        got = lax.ppermute(
            give,
            AXES,
            [((s + shift) % SEC * DP + d, s * DP + (d ^ bit)) for s in every for d in range(DP)],
        )
        part = keep.astype(F32) + got.astype(F32)
        if not shift:
            part = part.astype(BF)
    share = CH // DP
    kernel_part = jnp.transpose(part.reshape(9, share, 3, CH), (1, 2, 0, 3)).reshape(share, 27, CH)
    return (final[None], kernel_part[None])


def solution(mesh):
    return jax.shard_map(
        local,
        mesh=mesh,
        in_specs=(
            P("section", None, "dp", None, None),
            P("section", None, None, None, None, None),
            P(None, "dp", None, None),
        ),
        out_specs=(P("section", None, "dp", None, None), P("section", "dp", None, None)),
        check_vma=False,
    )
```

```python
import functools
import math

import jax
import jax.numpy as jnp
import numpy as np
from jax import lax
from jax.experimental import pallas as pl
from jax.experimental.pallas import tpu as pltpu
from jax.sharding import PartitionSpec as P

BF = jnp.bfloat16
F32 = jnp.float32
DP = 32
SEC = 8
FRAMES = 9
ROWS = 4
COLS = 32
CH = 128
AXES = ("section", "dp")
HALVING = (1, 2, 4, 8, 16)


def permute(value, hops):
    pairs = [
        (src * DP + d, dst * DP + d + off)
        for src, dst, off in hops
        for d in range(DP)
        if 0 <= d + off < DP
    ]
    return lax.ppermute(value, AXES, pairs)


def fill(x_ref, frame, row, value):
    count = value.shape[0] // COLS
    col = lax.broadcasted_iota(jnp.int32, value.shape, 0) % COLS
    size = value.shape[0]
    after = jnp.where(col == COLS - 1, 0.0, pltpu.roll(value, size - 1, 0))
    before = jnp.where(col == 0, 0.0, pltpu.roll(value, 1, 0))
    for n, part in enumerate((after, value, before)):
        x_ref[frame, row : row + count, :, n * CH : (n + 1) * CH] = part.astype(BF).reshape(
            count, COLS, CH
        )


def weights(w_ref):
    return jnp.concatenate(
        [
            jnp.concatenate(
                [w_ref[(9 * i + n) * CH : (9 * i + n + 1) * CH, :] for n in range(9)], axis=1
            )
            for i in range(3)
        ],
        axis=0,
    )


def back_pass(x_ref, rhs, slope_ref, rows, emit):
    group = 3
    size = rows * COLS
    one_later = None
    two_later = None
    for start in range(FRAMES - group, -1, -group):
        lhs = jnp.concatenate(
            [x_ref[start : start + group, 2 - j : 2 - j + rows] for j in range(3)], axis=-1
        ).reshape(group * size, 9 * CH)
        part = lax.dot_general(
            lhs, rhs, (((1,), (1,)), ((), ())), preferred_element_type=F32
        )
        for t in range(group - 1, -1, -1):
            here = part[t * size : (t + 1) * size]
            back = here[:, 2 * CH :]
            if one_later is not None:
                back = back + one_later[:, CH : 2 * CH]
            if two_later is not None:
                back = back + two_later[:, :CH]
            frame = start + t
            grad = x_ref[frame, 1 : 1 + rows, :, CH : 2 * CH].reshape(size, CH).astype(F32)
            new = grad + slope_ref[frame].reshape(size, CH) * back
            emit(frame, new.astype(BF))
            two_later = one_later
            one_later = here


def load(low_ref, own_ref, high_ref, x_ref):
    for t in range(FRAMES):
        whole = jnp.concatenate([low_ref[t], own_ref[t], high_ref[t]], axis=0)
        fill(x_ref, t, 0, whole.reshape(-1, CH).astype(F32))


def emit_to(refs):
    out_ref, top_ref, bottom_ref = refs
    edge = top_ref.shape[1]

    def emit(frame, value):
        whole = value.reshape(ROWS, COLS, CH)
        out_ref[frame] = whole
        top_ref[frame] = whole[:edge]
        bottom_ref[frame] = whole[ROWS - edge :]

    return emit


def single_kernel(low_ref, own_ref, high_ref, w_ref, slope_ref, *rest):
    *outs, x_ref = rest
    load(low_ref, own_ref, high_ref, x_ref)
    back_pass(x_ref, weights(w_ref), slope_ref, ROWS, emit_to(outs))


def wide_kernel(low_ref, own_ref, high_ref, w_ref, slope_ref, *rest):
    own_out, low_out, high_out, x_ref = rest
    load(low_ref, own_ref, high_ref, x_ref)

    def emit(frame, value):
        whole = value.reshape(ROWS + 2, COLS, CH)
        low_out[frame] = whole[:1]
        own_out[frame] = whole[1 : 1 + ROWS]
        high_out[frame] = whole[1 + ROWS :]

    back_pass(x_ref, weights(w_ref), slope_ref, ROWS + 2, emit)


def double_kernel(low_ref, own_ref, high_ref, w1_ref, slope1_ref, w0_ref, slope0_ref, *rest):
    *outs, middle_ref, x1_ref, x0_ref = rest
    load(low_ref, own_ref, high_ref, x1_ref)

    def emit_middle(frame, value):
        fill(x0_ref, frame, 0, value.astype(F32))
        middle_ref[frame] = value.reshape(ROWS + 2, COLS, CH)[1 : 1 + ROWS]

    back_pass(x1_ref, weights(w1_ref), slope1_ref, ROWS + 2, emit_middle)
    back_pass(x0_ref, weights(w0_ref), slope0_ref, ROWS, emit_to(outs))


def in_vmem(count):
    return [pl.BlockSpec(memory_space=pltpu.VMEM)] * count


def rows_shape(rows):
    return jax.ShapeDtypeStruct((FRAMES, rows, COLS, CH), BF)


def block_call(kernel, name, operands, outs, halos):
    return pl.pallas_call(
        kernel,
        out_shape=[rows_shape(r) for r in outs],
        in_specs=in_vmem(len(operands)),
        out_specs=in_vmem(len(outs)),
        scratch_shapes=[pltpu.VMEM((FRAMES, r, COLS, 3 * CH), BF) for r in halos],
        compiler_params=pltpu.CompilerParams(vmem_limit_bytes=24 << 20),
        name=name,
    )(*operands)


def single(low, own, high, w, slope, edge):
    return block_call(
        single_kernel,
        f"one_block_{edge}",
        (low, own, high, w, slope),
        (ROWS, edge, edge),
        (ROWS + 2,),
    )


def wide(low, own, high, w, slope):
    return block_call(
        wide_kernel,
        "wide_block",
        (low, own, high, w, slope),
        (ROWS, 1, 1),
        (ROWS + 4,),
    )


def double(low, own, high, w1, slope1, w0, slope0):
    return block_call(
        double_kernel,
        "two_blocks",
        (low, own, high, w1, slope1, w0, slope0),
        (ROWS, 2, 2, ROWS),
        (ROWS + 4, ROWS + 2),
    )


def tap_rows_kernel(act_ref, order_ref, out_ref, u_ref):
    for t in range(FRAMES):
        x = act_ref[t].reshape(-1, CH).astype(F32)
        u = (x * jax.nn.sigmoid(x)).astype(BF).astype(F32)
        col = lax.broadcasted_iota(jnp.int32, u.shape, 0) % COLS
        size = u.shape[0]
        before = jnp.where(col == 0, 0.0, pltpu.roll(u, 1, 0))
        after = jnp.where(col == COLS - 1, 0.0, pltpu.roll(u, size - 1, 0))
        for k, part in enumerate((before, u, after)):
            u_ref[k, t] = part.astype(BF).reshape(ROWS + 2, COLS, CH)
    for j in range(3):
        for k in range(3):
            taken = u_ref[k, :, j : j + ROWS].reshape(FRAMES * ROWS * COLS, CH)
            out_ref[3 * j + k] = lax.dot_general(
                order_ref[...], taken, (((1,), (1,)), ((), ())), preferred_element_type=F32
            ).astype(BF)


def tap_rows(act6, order):
    return pl.pallas_call(
        tap_rows_kernel,
        out_shape=jax.ShapeDtypeStruct((9, CH, FRAMES * ROWS * COLS), BF),
        in_specs=in_vmem(2),
        out_specs=pl.BlockSpec(memory_space=pltpu.VMEM),
        scratch_shapes=[pltpu.VMEM((3, FRAMES, ROWS + 2, COLS, CH), BF)],
        compiler_params=pltpu.CompilerParams(vmem_limit_bytes=24 << 20),
        name="tap_rows",
    )(act6, order)


def taps_kernel(scale, ut_ref, g_ref, out_ref):
    grad = g_ref[...].reshape(FRAMES, ROWS * COLS, CH)
    padded = jnp.concatenate([grad, jnp.zeros((2, ROWS * COLS, CH), BF)], axis=0)
    rhs = jnp.concatenate([padded[2 - i : 2 - i + FRAMES] for i in range(3)], axis=-1).reshape(
        FRAMES * ROWS * COLS, 3 * CH
    )
    for n in range(3):
        taps_here = slice(3 * n, 3 * n + 3)
        lhs = ut_ref[taps_here].reshape(3 * CH, FRAMES * ROWS * COLS)
        part = jnp.dot(lhs, rhs, preferred_element_type=F32)
        out_ref[taps_here] = (part * scale).astype(BF).reshape(3, CH, 3 * CH)


def taps(ut, grad, scale):
    return pl.pallas_call(
        functools.partial(taps_kernel, scale),
        out_shape=jax.ShapeDtypeStruct((9, CH, 3 * CH), BF),
        in_specs=in_vmem(2),
        out_specs=pl.BlockSpec(memory_space=pltpu.VMEM),
        compiler_params=pltpu.CompilerParams(vmem_limit_bytes=24 << 20),
        name="kernel_taps",
    )(ut, grad)


def channel_order():
    share = CH // DP
    order = []
    for n in range(CH):
        slot, rest = divmod(n, share)
        d = 0
        for place, bit in enumerate(HALVING):
            if (slot >> (len(HALVING) - 1 - place)) & 1:
                d |= bit
        order.append(d * share + rest)
    matrix = np.zeros((CH, CH), np.float32)
    matrix[np.arange(CH), order] = 1.0
    return matrix


def slope_of(x):
    x = x.astype(F32)
    sig = jax.nn.sigmoid(x)
    return sig * (1.0 + x * (1.0 - sig))


def local(acts, kernels, cotangent):
    me = lax.axis_index("section")
    dp = lax.axis_index("dp")
    scale = 1.0 / math.sqrt(FRAMES * ROWS * DP * COLS)
    every = range(SEC)
    pairs = (4, 2, 0)
    barrier = lax.optimization_barrier

    def blank(rows):
        return jnp.zeros((FRAMES, rows, COLS, CH), BF)

    both = jnp.concatenate([cotangent, acts[0]], axis=0)
    edge_low = permute(both[:, -1:], [(s, s, 1) for s in every])
    edge_high = permute(both[:, :1], [(s, s, -1) for s in every])
    low0, high0 = edge_low[:FRAMES], edge_high[:FRAMES]
    act6 = jnp.concatenate([edge_low[FRAMES:], acts[0], edge_high[FRAMES:]], axis=1)

    w = kernels[0].reshape(27 * CH, CH)
    slope = slope_of(acts[0])
    result, top, bottom = lax.cond(
        me == 7,
        lambda: tuple(single(low0, cotangent, high0, w, slope, 1)),
        lambda: (blank(ROWS), blank(1), blank(1)),
    )

    def hop(result, top, bottom, source, target):
        own = permute(result, [(source, target, 0)])
        low = permute(bottom, [(source, target, 1)])
        high = permute(top, [(source, target, -1)])
        return low, own, high

    w_next = permute(w, [(s + 1, s, 0) for s in pairs])
    act6, result = barrier((act6, result))
    act_next = permute(act6, [(s + 1, s, 0) for s in pairs])
    row = lax.broadcasted_iota(jnp.int32, act_next.shape, 1) + dp * ROWS - 1
    inside = (row >= 0) & (row < DP * ROWS)
    slope_next = jnp.where(inside, slope_of(act_next), 0.0)

    low, own, high = hop(result, top, bottom, 7, 6)
    result, top, bottom = lax.cond(
        me == 6,
        lambda: tuple(single(low, own, high, w, slope, 2)),
        lambda: (result, blank(2), blank(2)),
    )
    act6, own, result = barrier((act6, own, result))
    grad = jnp.where(me == 7, cotangent, own)
    ut = tap_rows(act6, jnp.asarray(channel_order(), BF))

    low, own, high = hop(result, top, bottom, 6, 4)
    ut, grad, low = barrier((ut, grad, low))
    for section in (4, 2):
        result, top, bottom, grad = lax.cond(
            me == section,
            lambda low=low, own=own, high=high: tuple(
                double(low, own, high, w_next, slope_next, w, slope)
            ),
            lambda result=result, top=top, bottom=bottom, grad=grad: (
                result,
                top,
                bottom,
                grad,
            ),
        )
        low, own, high = hop(result, top, bottom, section, section - 2)

    grad = grad + permute(result, [(s + 1, s, 0) for s in (5, 3, 1)])
    grad, low = barrier((grad, low))

    grad, low, high = lax.cond(
        me == 0,
        lambda: tuple(wide(low, own, high, w_next, slope_next)),
        lambda: (grad, blank(1), blank(1)),
    )
    part = taps(ut, grad, scale)
    grad, low, high, part = barrier((grad, low, high, part))
    result = result + permute(grad, [(s - 1, s, 0) for s in (5, 3, 1)])
    final = lax.cond(
        me == 0,
        lambda: single(low, grad, high, w, slope, 1)[0],
        lambda: result,
    )

    for bit in HALVING:
        size = part.shape[1] // 2
        mine = (dp // bit) % 2
        keep = lax.dynamic_slice_in_dim(part, mine * size, size, 1)
        give = lax.dynamic_slice_in_dim(part, (1 - mine) * size, size, 1)
        got = lax.ppermute(
            give, AXES, [(s * DP + d, s * DP + (d ^ bit)) for s in every for d in range(DP)]
        )
        part = keep.astype(F32) + got.astype(F32)
        if bit != HALVING[-1]:
            part = part.astype(BF)
    share = CH // DP
    kernel_part = jnp.transpose(part.reshape(9, share, 3, CH), (1, 2, 0, 3)).reshape(share, 27, CH)
    return (final[None], kernel_part[None])


def solution(mesh):
    return jax.shard_map(
        local,
        mesh=mesh,
        in_specs=(
            P("section", None, "dp", None, None),
            P("section", None, None, None, None, None),
            P(None, "dp", None, None),
        ),
        out_specs=(P("section", None, "dp", None, None), P("section", "dp", None, None)),
        check_vma=False,
    )
```

```python
import functools
import math

import jax
import jax.numpy as jnp
import numpy as np
from jax import lax
from jax.experimental import pallas as pl
from jax.experimental.pallas import tpu as pltpu
from jax.sharding import Mesh
from jax.sharding import PartitionSpec as P

BF = jnp.bfloat16
F32 = jnp.float32
DP = 32
SEC = 8
FRAMES = 9
ROWS = 4
COLS = 32
CH = 128
PEERS = 16
AXES = ("section", "z", "y", "core")


def permute(value, hops):
    pairs = [
        (src * DP + d, dst * DP + d + off)
        for src, dst, off in hops
        for d in range(DP)
        if 0 <= d + off < DP
    ]
    return lax.ppermute(value, AXES, pairs)


def fill(x_ref, frame, row, value):
    count = value.shape[0] // COLS
    col = lax.broadcasted_iota(jnp.int32, value.shape, 0) % COLS
    size = value.shape[0]
    after = jnp.where(col == COLS - 1, 0.0, pltpu.roll(value, size - 1, 0))
    before = jnp.where(col == 0, 0.0, pltpu.roll(value, 1, 0))
    for n, part in enumerate((after, value, before)):
        x_ref[frame, row : row + count, :, n * CH : (n + 1) * CH] = part.astype(BF).reshape(
            count, COLS, CH
        )


def weights(w_ref):
    return jnp.concatenate(
        [
            jnp.concatenate(
                [w_ref[(9 * i + n) * CH : (9 * i + n + 1) * CH, :] for n in range(9)], axis=1
            )
            for i in range(3)
        ],
        axis=0,
    )


def back_pass(x_ref, rhs, slope_ref, rows, emit, rhs_dim=1):
    group = 3
    size = rows * COLS
    one_later = None
    two_later = None
    for start in range(FRAMES - group, -1, -group):
        lhs = jnp.concatenate(
            [x_ref[start : start + group, 2 - j : 2 - j + rows] for j in range(3)], axis=-1
        ).reshape(group * size, 9 * CH)
        part = lax.dot_general(
            lhs, rhs, (((1,), (rhs_dim,)), ((), ())), preferred_element_type=F32
        )
        for t in range(group - 1, -1, -1):
            here = part[t * size : (t + 1) * size]
            back = here[:, 2 * CH :]
            if one_later is not None:
                back = back + one_later[:, CH : 2 * CH]
            if two_later is not None:
                back = back + two_later[:, :CH]
            frame = start + t
            grad = x_ref[frame, 1 : 1 + rows, :, CH : 2 * CH].reshape(size, CH).astype(F32)
            new = grad + slope_ref[frame].reshape(size, CH) * back
            emit(frame, new.astype(BF))
            two_later = one_later
            one_later = here


def load(low_ref, own_ref, high_ref, x_ref):
    for t in range(FRAMES):
        whole = jnp.concatenate([low_ref[t], own_ref[t], high_ref[t]], axis=0)
        fill(x_ref, t, 0, whole.reshape(-1, CH).astype(F32))


def emit_to(refs):
    out_ref, top_ref, bottom_ref = refs
    edge = top_ref.shape[1]

    def emit(frame, value):
        whole = value.reshape(ROWS, COLS, CH)
        out_ref[frame] = whole
        top_ref[frame] = whole[:edge]
        bottom_ref[frame] = whole[ROWS - edge :]

    return emit


def single_kernel(low_ref, own_ref, high_ref, slope_ref, w_ref, *rest):
    *outs, x_ref, held_ref, sem = rest
    copy = pltpu.make_async_copy(w_ref, held_ref, sem)
    copy.start()
    load(low_ref, own_ref, high_ref, x_ref)
    copy.wait()
    back_pass(x_ref, weights(held_ref), slope_ref, ROWS, emit_to(outs))


def last_kernel(low_ref, own_ref, high_ref, slope_ref, w_ref, out_ref, x_ref):
    load(low_ref, own_ref, high_ref, x_ref)

    def emit(frame, value):
        out_ref[frame] = value.reshape(ROWS, COLS, CH)

    back_pass(x_ref, w_ref[...], slope_ref, ROWS, emit, 0)


def wide_kernel(low_ref, own_ref, high_ref, w_ref, slope_ref, *rest):
    own_out, low_out, high_out, x_ref = rest
    load(low_ref, own_ref, high_ref, x_ref)

    def emit(frame, value):
        whole = value.reshape(ROWS + 2, COLS, CH)
        low_out[frame] = whole[:1]
        own_out[frame] = whole[1 : 1 + ROWS]
        high_out[frame] = whole[1 + ROWS :]

    back_pass(x_ref, w_ref[...], slope_ref, ROWS + 2, emit, 0)


def double_kernel(low_ref, own_ref, high_ref, w1_ref, slope1_ref, w0_ref, slope0_ref, *rest):
    *outs, middle_ref, x1_ref, x0_ref = rest
    load(low_ref, own_ref, high_ref, x1_ref)

    def emit_middle(frame, value):
        fill(x0_ref, frame, 0, value.astype(F32))
        middle_ref[frame] = value.reshape(ROWS + 2, COLS, CH)[1 : 1 + ROWS]

    back_pass(x1_ref, w1_ref[...], slope1_ref, ROWS + 2, emit_middle, 0)
    back_pass(x0_ref, w0_ref[...], slope0_ref, ROWS, emit_to(outs), 0)


def in_vmem(count):
    return [pl.BlockSpec(memory_space=pltpu.VMEM)] * count


def rows_shape(rows):
    return jax.ShapeDtypeStruct((FRAMES, rows, COLS, CH), BF)


def block_call(kernel, name, operands, outs, halos, held=None):
    scratch = [pltpu.VMEM((FRAMES, r, COLS, 3 * CH), BF) for r in halos]
    specs = in_vmem(len(operands))
    if held is not None:
        operands = (*operands, held)
        specs.append(pl.BlockSpec(memory_space=pl.ANY))
        scratch += [pltpu.VMEM(held.shape, BF), pltpu.SemaphoreType.DMA]
    return pl.pallas_call(
        kernel,
        out_shape=[rows_shape(r) for r in outs],
        in_specs=specs,
        out_specs=in_vmem(len(outs)),
        scratch_shapes=scratch,
        compiler_params=pltpu.CompilerParams(vmem_limit_bytes=24 << 20),
        name=name,
    )(*operands)


def single(low, own, high, w, slope, edge):
    return block_call(
        single_kernel,
        f"one_block_{edge}",
        (low, own, high, slope),
        (ROWS, edge, edge),
        (ROWS + 2,),
        w,
    )


def last(low, own, high, w, slope):
    return block_call(
        last_kernel, "last_block", (low, own, high, slope, w), (ROWS,), (ROWS + 2,)
    )[0]


def wide(low, own, high, w, slope):
    return block_call(
        wide_kernel,
        "wide_block",
        (low, own, high, w, slope),
        (ROWS, 1, 1),
        (ROWS + 4,),
    )


def double(low, own, high, w1, slope1, w0, slope0):
    return block_call(
        double_kernel,
        "two_blocks",
        (low, own, high, w1, slope1, w0, slope0),
        (ROWS, 2, 2, ROWS),
        (ROWS + 4, ROWS + 2),
    )


def tap_rows_kernel(act_ref, order_ref, out_ref, u_ref):
    for t in range(FRAMES):
        x = act_ref[t].reshape(-1, CH).astype(F32)
        u = (x * jax.nn.sigmoid(x)).astype(BF).astype(F32)
        col = lax.broadcasted_iota(jnp.int32, u.shape, 0) % COLS
        size = u.shape[0]
        before = jnp.where(col == 0, 0.0, pltpu.roll(u, 1, 0))
        after = jnp.where(col == COLS - 1, 0.0, pltpu.roll(u, size - 1, 0))
        for k, part in enumerate((before, u, after)):
            u_ref[k, t] = part.astype(BF).reshape(ROWS + 2, COLS, CH)
    for j in range(3):
        for k in range(3):
            taken = u_ref[k, :, j : j + ROWS].reshape(FRAMES * ROWS * COLS, CH)
            out_ref[3 * j + k] = lax.dot_general(
                order_ref[...], taken, (((1,), (1,)), ((), ())), preferred_element_type=F32
            ).astype(BF)


def tap_rows(act6, order):
    return pl.pallas_call(
        tap_rows_kernel,
        out_shape=jax.ShapeDtypeStruct((9, CH, FRAMES * ROWS * COLS), BF),
        in_specs=in_vmem(2),
        out_specs=pl.BlockSpec(memory_space=pltpu.VMEM),
        scratch_shapes=[pltpu.VMEM((3, FRAMES, ROWS + 2, COLS, CH), BF)],
        compiler_params=pltpu.CompilerParams(vmem_limit_bytes=24 << 20),
        name="tap_rows",
    )(act6, order)


def taps_kernel(scale, ut_ref, g_ref, out_ref):
    grad = g_ref[...].reshape(FRAMES, ROWS * COLS, CH)
    padded = jnp.concatenate([grad, jnp.zeros((2, ROWS * COLS, CH), BF)], axis=0)
    rhs = jnp.concatenate([padded[2 - i : 2 - i + FRAMES] for i in range(3)], axis=-1).reshape(
        FRAMES * ROWS * COLS, 3 * CH
    )
    for n in range(3):
        taps_here = slice(3 * n, 3 * n + 3)
        lhs = ut_ref[taps_here].reshape(3 * CH, FRAMES * ROWS * COLS)
        part = jnp.dot(lhs, rhs, preferred_element_type=F32)
        out_ref[taps_here] = (part * scale).astype(BF).reshape(3, CH, 3 * CH)


def taps(ut, grad, scale):
    return pl.pallas_call(
        functools.partial(taps_kernel, scale),
        out_shape=jax.ShapeDtypeStruct((9, CH, 3 * CH), BF),
        in_specs=in_vmem(2),
        out_specs=pl.BlockSpec(memory_space=pltpu.VMEM),
        compiler_params=pltpu.CompilerParams(vmem_limit_bytes=24 << 20),
        name="kernel_taps",
    )(ut, grad)


def channel_order():
    share = CH // DP
    order = [
        (chip * 2 + core) * share + rest
        for core in range(2)
        for chip in range(PEERS)
        for rest in range(share)
    ]
    matrix = np.zeros((CH, CH), np.float32)
    matrix[np.arange(CH), order] = 1.0
    return matrix


def slope_of(x):
    x = x.astype(F32)
    sig = jax.nn.sigmoid(x)
    return sig * (1.0 + x * (1.0 - sig))


def as_matrix(w):
    kern = w.reshape(3, 3, 3, CH, CH)
    return jnp.transpose(kern, (1, 2, 4, 0, 3)).reshape(9 * CH, 3 * CH)


def local(acts, kernels, cotangent):
    me = lax.axis_index("section")
    dp = lax.axis_index(AXES[1:])
    core = lax.axis_index("core")
    scale = 1.0 / math.sqrt(FRAMES * ROWS * DP * COLS)
    every = range(SEC)
    pairs = (4, 2, 0)
    barrier = lax.optimization_barrier

    def blank(rows):
        return jnp.zeros((FRAMES, rows, COLS, CH), BF)

    both = jnp.concatenate([cotangent, acts[0]], axis=0)
    edge_low = permute(both[:, -1:], [(s, s, 1) for s in every])
    edge_high = permute(both[:, :1], [(s, s, -1) for s in every])
    low0, high0 = edge_low[:FRAMES], edge_high[:FRAMES]
    act6 = jnp.concatenate([edge_low[FRAMES:], acts[0], edge_high[FRAMES:]], axis=1)

    w = kernels[0].reshape(27 * CH, CH)
    slope = slope_of(acts[0])
    result, top, bottom = lax.cond(
        me == 7,
        lambda: tuple(single(low0, cotangent, high0, w, slope, 1)),
        lambda: (blank(ROWS), blank(1), blank(1)),
    )

    def hop(result, top, bottom, source, target):
        own = permute(result, [(source, target, 0)])
        low = permute(bottom, [(source, target, 1)])
        high = permute(top, [(source, target, -1)])
        return low, own, high

    w_next = permute(w, [(s + 1, s, 0) for s in pairs])
    act6, result = barrier((act6, result))
    act_next = permute(act6, [(s + 1, s, 0) for s in pairs])
    row = lax.broadcasted_iota(jnp.int32, act_next.shape, 1) + dp * ROWS - 1
    inside = (row >= 0) & (row < DP * ROWS)
    slope_next = jnp.where(inside, slope_of(act_next), 0.0)

    low, own, high = hop(result, top, bottom, 7, 6)
    result, top, bottom = lax.cond(
        me == 6,
        lambda: tuple(single(low, own, high, w, slope, 2)),
        lambda: (result, blank(2), blank(2)),
    )
    w, own, result = barrier((w, own, result))
    grad = jnp.where(me == 7, cotangent, own)
    w_next, w = as_matrix(w_next), as_matrix(w)

    low, own, high = hop(result, top, bottom, 6, 4)
    w, w_next, grad, low = barrier((w, w_next, grad, low))
    for section in (4, 2):
        result, top, bottom, grad = lax.cond(
            me == section,
            lambda low=low, own=own, high=high: tuple(
                double(low, own, high, w_next, slope_next, w, slope)
            ),
            lambda result=result, top=top, bottom=bottom, grad=grad: (
                result,
                top,
                bottom,
                grad,
            ),
        )
        low, own, high = hop(result, top, bottom, section, section - 2)

    grad = grad + permute(result, [(s + 1, s, 0) for s in (5, 3, 1)])
    act6, grad = barrier((act6, grad))
    ut = tap_rows(act6, jnp.asarray(channel_order(), BF))
    ut, grad, low = barrier((ut, grad, low))

    grad, low, high = lax.cond(
        me == 0,
        lambda: tuple(wide(low, own, high, w_next, slope_next)),
        lambda: (grad, blank(1), blank(1)),
    )
    part = taps(ut, grad, scale)
    grad, low, high, part = barrier((grad, low, high, part))
    result = result + permute(grad, [(s - 1, s, 0) for s in (5, 3, 1)])
    final = lax.cond(
        me == 0,
        lambda: last(low, grad, high, w, slope),
        lambda: result,
    )

    half = CH // 2
    keep = lax.dynamic_slice_in_dim(part, core * half, half, 1)
    give = lax.dynamic_slice_in_dim(part, (1 - core) * half, half, 1)
    got = lax.ppermute(
        give, AXES, [(s * DP + d, s * DP + (d ^ 1)) for s in every for d in range(DP)]
    )
    part = (keep.astype(F32) + got.astype(F32)).astype(BF)
    part = jnp.transpose(part.reshape(9, PEERS, CH // DP, 3 * CH), (1, 0, 2, 3))
    part = lax.all_to_all(part, ("z", "y"), 0, 0, tiled=True)
    part = jnp.sum(part.astype(F32), axis=0)
    share = CH // DP
    kernel_part = jnp.transpose(part.reshape(9, share, 3, CH), (1, 2, 0, 3)).reshape(share, 27, CH)
    return (final[None], kernel_part[None])


def solution(mesh):
    parts = Mesh(mesh.devices.reshape(SEC, DP // 4, 2, 2), AXES)
    rows = AXES[1:]
    return jax.shard_map(
        local,
        mesh=parts,
        in_specs=(
            P("section", None, rows, None, None),
            P("section", None, None, None, None, None),
            P(None, rows, None, None),
        ),
        out_specs=(P("section", None, rows, None, None), P("section", rows, None, None)),
        check_vma=False,
    )
```

```python
import functools
import math

import jax
import jax.numpy as jnp
import numpy as np
from jax import lax
from jax.experimental import pallas as pl
from jax.experimental.pallas import tpu as pltpu
from jax.sharding import Mesh
from jax.sharding import PartitionSpec as P

BF = jnp.bfloat16
F32 = jnp.float32
DP = 32
SEC = 8
FRAMES = 9
ROWS = 4
COLS = 32
CH = 128
PEERS = 16
AXES = ("section", "z", "y", "core")


def permute(value, hops):
    pairs = [
        (src * DP + d, dst * DP + d + off)
        for src, dst, off in hops
        for d in range(DP)
        if 0 <= d + off < DP
    ]
    return lax.ppermute(value, AXES, pairs)


def fill(x_ref, frame, row, value):
    count = value.shape[0] // COLS
    col = lax.broadcasted_iota(jnp.int32, value.shape, 0) % COLS
    size = value.shape[0]
    after = jnp.where(col == COLS - 1, 0.0, pltpu.roll(value, size - 1, 0))
    before = jnp.where(col == 0, 0.0, pltpu.roll(value, 1, 0))
    for n, part in enumerate((after, value, before)):
        x_ref[frame, row : row + count, :, n * CH : (n + 1) * CH] = part.astype(BF).reshape(
            count, COLS, CH
        )


def weights(w_ref):
    return jnp.concatenate(
        [
            jnp.concatenate(
                [w_ref[(9 * i + n) * CH : (9 * i + n + 1) * CH, :] for n in range(9)], axis=1
            )
            for i in range(3)
        ],
        axis=0,
    )


def back_pass(x_ref, rhs, slope_ref, rows, emit):
    group = 3
    size = rows * COLS
    one_later = None
    two_later = None
    for start in range(FRAMES - group, -1, -group):
        lhs = jnp.concatenate(
            [x_ref[start : start + group, 2 - j : 2 - j + rows] for j in range(3)], axis=-1
        ).reshape(group * size, 9 * CH)
        part = lax.dot_general(
            lhs, rhs, (((1,), (1,)), ((), ())), preferred_element_type=F32
        )
        for t in range(group - 1, -1, -1):
            here = part[t * size : (t + 1) * size]
            back = here[:, 2 * CH :]
            if one_later is not None:
                back = back + one_later[:, CH : 2 * CH]
            if two_later is not None:
                back = back + two_later[:, :CH]
            frame = start + t
            grad = x_ref[frame, 1 : 1 + rows, :, CH : 2 * CH].reshape(size, CH).astype(F32)
            new = grad + slope_ref[frame].reshape(size, CH) * back
            emit(frame, new.astype(BF))
            two_later = one_later
            one_later = here


def load(low_ref, own_ref, high_ref, x_ref):
    for t in range(FRAMES):
        whole = jnp.concatenate([low_ref[t], own_ref[t], high_ref[t]], axis=0)
        fill(x_ref, t, 0, whole.reshape(-1, CH).astype(F32))


def emit_to(refs):
    out_ref, top_ref, bottom_ref = refs
    edge = top_ref.shape[1]

    def emit(frame, value):
        whole = value.reshape(ROWS, COLS, CH)
        out_ref[frame] = whole
        top_ref[frame] = whole[:edge]
        bottom_ref[frame] = whole[ROWS - edge :]

    return emit


def single_kernel(low_ref, own_ref, high_ref, slope_ref, w_ref, *rest):
    *outs, x_ref, held_ref, sem = rest
    copy = pltpu.make_async_copy(w_ref, held_ref, sem)
    copy.start()
    load(low_ref, own_ref, high_ref, x_ref)
    copy.wait()
    back_pass(x_ref, weights(held_ref), slope_ref, ROWS, emit_to(outs))


def last_kernel(low_ref, own_ref, high_ref, slope_ref, w_ref, out_ref, x_ref):
    load(low_ref, own_ref, high_ref, x_ref)

    def emit(frame, value):
        out_ref[frame] = value.reshape(ROWS, COLS, CH)

    back_pass(x_ref, weights(w_ref), slope_ref, ROWS, emit)


def wide_kernel(low_ref, own_ref, high_ref, w_ref, slope_ref, *rest):
    own_out, low_out, high_out, x_ref = rest
    load(low_ref, own_ref, high_ref, x_ref)

    def emit(frame, value):
        whole = value.reshape(ROWS + 2, COLS, CH)
        low_out[frame] = whole[:1]
        own_out[frame] = whole[1 : 1 + ROWS]
        high_out[frame] = whole[1 + ROWS :]

    back_pass(x_ref, weights(w_ref), slope_ref, ROWS + 2, emit)


def double_kernel(low_ref, own_ref, high_ref, w1_ref, slope1_ref, w0_ref, slope0_ref, *rest):
    *outs, middle_ref, x1_ref, x0_ref = rest
    load(low_ref, own_ref, high_ref, x1_ref)

    def emit_middle(frame, value):
        fill(x0_ref, frame, 0, value.astype(F32))
        middle_ref[frame] = value.reshape(ROWS + 2, COLS, CH)[1 : 1 + ROWS]

    back_pass(x1_ref, weights(w1_ref), slope1_ref, ROWS + 2, emit_middle)
    back_pass(x0_ref, weights(w0_ref), slope0_ref, ROWS, emit_to(outs))


def in_vmem(count):
    return [pl.BlockSpec(memory_space=pltpu.VMEM)] * count


def rows_shape(rows):
    return jax.ShapeDtypeStruct((FRAMES, rows, COLS, CH), BF)


def block_call(kernel, name, operands, outs, halos, held=None):
    scratch = [pltpu.VMEM((FRAMES, r, COLS, 3 * CH), BF) for r in halos]
    specs = in_vmem(len(operands))
    if held is not None:
        operands = (*operands, held)
        specs.append(pl.BlockSpec(memory_space=pl.ANY))
        scratch += [pltpu.VMEM(held.shape, BF), pltpu.SemaphoreType.DMA]
    return pl.pallas_call(
        kernel,
        out_shape=[rows_shape(r) for r in outs],
        in_specs=specs,
        out_specs=in_vmem(len(outs)),
        scratch_shapes=scratch,
        compiler_params=pltpu.CompilerParams(vmem_limit_bytes=24 << 20),
        name=name,
    )(*operands)


def single(low, own, high, w, slope, edge):
    return block_call(
        single_kernel,
        f"one_block_{edge}",
        (low, own, high, slope),
        (ROWS, edge, edge),
        (ROWS + 2,),
        w,
    )


def last(low, own, high, w, slope):
    return block_call(
        last_kernel, "last_block", (low, own, high, slope, w), (ROWS,), (ROWS + 2,)
    )[0]


def wide(low, own, high, w, slope):
    return block_call(
        wide_kernel,
        "wide_block",
        (low, own, high, w, slope),
        (ROWS, 1, 1),
        (ROWS + 4,),
    )


def double(low, own, high, w1, slope1, w0, slope0):
    return block_call(
        double_kernel,
        "two_blocks",
        (low, own, high, w1, slope1, w0, slope0),
        (ROWS, 2, 2, ROWS),
        (ROWS + 4, ROWS + 2),
    )


def tap_rows_kernel(act_ref, order_ref, out_ref, u_ref):
    for t in range(FRAMES):
        x = act_ref[t].reshape(-1, CH).astype(F32)
        u = (x * jax.nn.sigmoid(x)).astype(BF).astype(F32)
        col = lax.broadcasted_iota(jnp.int32, u.shape, 0) % COLS
        size = u.shape[0]
        before = jnp.where(col == 0, 0.0, pltpu.roll(u, 1, 0))
        after = jnp.where(col == COLS - 1, 0.0, pltpu.roll(u, size - 1, 0))
        for k, part in enumerate((before, u, after)):
            u_ref[k, t] = part.astype(BF).reshape(ROWS + 2, COLS, CH)
    for j in range(3):
        for k in range(3):
            taken = u_ref[k, :, j : j + ROWS].reshape(FRAMES * ROWS * COLS, CH)
            out_ref[3 * j + k] = lax.dot_general(
                order_ref[...], taken, (((1,), (1,)), ((), ())), preferred_element_type=F32
            ).astype(BF)


def tap_rows(act6, order):
    return pl.pallas_call(
        tap_rows_kernel,
        out_shape=jax.ShapeDtypeStruct((9, CH, FRAMES * ROWS * COLS), BF),
        in_specs=in_vmem(2),
        out_specs=pl.BlockSpec(memory_space=pltpu.VMEM),
        scratch_shapes=[pltpu.VMEM((3, FRAMES, ROWS + 2, COLS, CH), BF)],
        compiler_params=pltpu.CompilerParams(vmem_limit_bytes=24 << 20),
        name="tap_rows",
    )(act6, order)


def taps_kernel(scale, ut_ref, g_ref, more_ref, out_ref):
    grad = (g_ref[...] + more_ref[...]).reshape(FRAMES, ROWS * COLS, CH)
    padded = jnp.concatenate([grad, jnp.zeros((2, ROWS * COLS, CH), BF)], axis=0)
    rhs = jnp.concatenate([padded[2 - i : 2 - i + FRAMES] for i in range(3)], axis=-1).reshape(
        FRAMES * ROWS * COLS, 3 * CH
    )
    for n in range(3):
        taps_here = slice(3 * n, 3 * n + 3)
        lhs = ut_ref[taps_here].reshape(3 * CH, FRAMES * ROWS * COLS)
        part = jnp.dot(lhs, rhs, preferred_element_type=F32)
        out_ref[taps_here] = (part * scale).astype(BF).reshape(3, CH, 3 * CH)


def taps(ut, grad, more, scale):
    return pl.pallas_call(
        functools.partial(taps_kernel, scale),
        out_shape=jax.ShapeDtypeStruct((9, CH, 3 * CH), BF),
        in_specs=in_vmem(3),
        out_specs=pl.BlockSpec(memory_space=pltpu.VMEM),
        compiler_params=pltpu.CompilerParams(vmem_limit_bytes=24 << 20),
        name="kernel_taps",
    )(ut, grad, more)


def channel_order():
    share = CH // DP
    order = [
        (chip * 2 + core) * share + rest
        for core in range(2)
        for chip in range(PEERS)
        for rest in range(share)
    ]
    matrix = np.zeros((CH, CH), np.float32)
    matrix[np.arange(CH), order] = 1.0
    return matrix


def slope_of(x):
    x = x.astype(F32)
    sig = jax.nn.sigmoid(x)
    return sig * (1.0 + x * (1.0 - sig))


def local(acts, kernels, cotangent):
    me = lax.axis_index("section")
    dp = lax.axis_index(AXES[1:])
    core = lax.axis_index("core")
    scale = 1.0 / math.sqrt(FRAMES * ROWS * DP * COLS)
    every = range(SEC)
    pairs = (4, 2, 0)
    barrier = lax.optimization_barrier

    def blank(rows):
        return jnp.zeros((FRAMES, rows, COLS, CH), BF)

    both = jnp.concatenate([cotangent, acts[0]], axis=0)
    edge_low = permute(both[:, -1:], [(s, s, 1) for s in every])
    edge_high = permute(both[:, :1], [(s, s, -1) for s in every])
    low0, high0 = edge_low[:FRAMES], edge_high[:FRAMES]
    act6 = jnp.concatenate([edge_low[FRAMES:], acts[0], edge_high[FRAMES:]], axis=1)

    w = kernels[0].reshape(27 * CH, CH)
    slope = slope_of(acts[0])
    result, top, bottom = lax.cond(
        me == 7,
        lambda: tuple(single(low0, cotangent, high0, w, slope, 1)),
        lambda: (blank(ROWS), blank(1), blank(1)),
    )

    def hop(result, top, bottom, source, target):
        own = permute(result, [(source, target, 0)])
        low = permute(bottom, [(source, target, 1)])
        high = permute(top, [(source, target, -1)])
        return low, own, high

    w_next = permute(w, [(s + 1, s, 0) for s in pairs])
    act6, result = barrier((act6, result))
    act_next = permute(act6, [(s + 1, s, 0) for s in pairs])
    row = lax.broadcasted_iota(jnp.int32, act_next.shape, 1) + dp * ROWS - 1
    inside = (row >= 0) & (row < DP * ROWS)
    slope_next = jnp.where(inside, slope_of(act_next), 0.0)

    low, own, high = hop(result, top, bottom, 7, 6)
    result, top, bottom = lax.cond(
        me == 6,
        lambda: tuple(single(low, own, high, w, slope, 2)),
        lambda: (result, blank(2), blank(2)),
    )
    own, result = barrier((own, result))
    grad = jnp.where(me == 7, cotangent, own)

    low, own, high = hop(result, top, bottom, 6, 4)
    grad, low = barrier((grad, low))
    came = own
    for section in (4, 2):
        result, top, bottom, grad = lax.cond(
            me == section,
            lambda low=low, own=own, high=high: tuple(
                double(low, own, high, w_next, slope_next, w, slope)
            ),
            lambda result=result, top=top, bottom=bottom, grad=grad: (
                result,
                top,
                bottom,
                grad,
            ),
        )
        low, own, high = hop(result, top, bottom, section, section - 2)
        if section == 4:
            came = came + own
    act6, grad, came = barrier((act6, grad, came))
    ut = tap_rows(act6, jnp.asarray(channel_order(), BF))
    ut, grad, low, own, high, came = barrier((ut, grad, low, own, high, came))

    forward = [(s - 1, s, 0) for s in (5, 3, 1)]
    passed = permute(came + own, forward)

    grad, low, high = lax.cond(
        me == 0,
        lambda: tuple(wide(low, own, high, w_next, slope_next)),
        lambda: (grad, blank(1), blank(1)),
    )
    part = taps(ut, grad, passed, scale)
    grad, low, high, part = barrier((grad, low, high, part))
    result = result + permute(grad, forward)
    final = lax.cond(
        me == 0,
        lambda: last(low, grad, high, w, slope),
        lambda: result,
    )

    half = CH // 2
    keep = lax.dynamic_slice_in_dim(part, core * half, half, 1)
    give = lax.dynamic_slice_in_dim(part, (1 - core) * half, half, 1)
    got = lax.ppermute(
        give, AXES, [(s * DP + d, s * DP + (d ^ 1)) for s in every for d in range(DP)]
    )
    part = (keep.astype(F32) + got.astype(F32)).astype(BF)
    part = jnp.transpose(part.reshape(9, PEERS, CH // DP, 3 * CH), (1, 0, 2, 3))
    part = lax.all_to_all(part, ("z", "y"), 0, 0, tiled=True)
    part = jnp.sum(part.astype(F32), axis=0)
    share = CH // DP
    kernel_part = jnp.transpose(part.reshape(9, share, 3, CH), (1, 2, 0, 3)).reshape(share, 27, CH)
    return (final[None], kernel_part[None])


def solution(mesh):
    parts = Mesh(mesh.devices.reshape(SEC, DP // 4, 2, 2), AXES)
    rows = AXES[1:]
    return jax.shard_map(
        local,
        mesh=parts,
        in_specs=(
            P("section", None, rows, None, None),
            P("section", None, None, None, None, None),
            P(None, rows, None, None),
        ),
        out_specs=(P("section", None, rows, None, None), P("section", rows, None, None)),
        check_vma=False,
    )
```

```python
import functools
import math

import jax
import jax.numpy as jnp
import numpy as np
from jax import lax
from jax.experimental import pallas as pl
from jax.experimental.pallas import tpu as pltpu
from jax.sharding import Mesh
from jax.sharding import PartitionSpec as P

BF = jnp.bfloat16
F32 = jnp.float32
DP = 32
SEC = 8
FRAMES = 9
ROWS = 4
COLS = 32
CH = 128
PEERS = 16
AXES = ("section", "z", "y", "core")


def permute(value, hops):
    pairs = [
        (src * DP + d, dst * DP + d + off)
        for src, dst, off in hops
        for d in range(DP)
        if 0 <= d + off < DP
    ]
    return lax.ppermute(value, AXES, pairs)


def fill(x_ref, frame, row, value):
    count = value.shape[0] // COLS
    col = lax.broadcasted_iota(jnp.int32, value.shape, 0) % COLS
    size = value.shape[0]
    after = jnp.where(col == COLS - 1, 0.0, pltpu.roll(value, size - 1, 0))
    before = jnp.where(col == 0, 0.0, pltpu.roll(value, 1, 0))
    for n, part in enumerate((after, value, before)):
        x_ref[frame, row : row + count, :, n * CH : (n + 1) * CH] = part.astype(BF).reshape(
            count, COLS, CH
        )


def weights(w_ref):
    return jnp.concatenate(
        [
            jnp.concatenate(
                [w_ref[(9 * i + n) * CH : (9 * i + n + 1) * CH, :] for n in range(9)], axis=1
            )
            for i in range(3)
        ],
        axis=0,
    )


def back_pass(x_ref, rhs, slope_ref, rows, emit):
    group = 3
    size = rows * COLS
    one_later = None
    two_later = None
    for start in range(FRAMES - group, -1, -group):
        lhs = jnp.concatenate(
            [x_ref[start : start + group, 2 - j : 2 - j + rows] for j in range(3)], axis=-1
        ).reshape(group * size, 9 * CH)
        part = lax.dot_general(
            lhs, rhs, (((1,), (1,)), ((), ())), preferred_element_type=F32
        )
        for t in range(group - 1, -1, -1):
            here = part[t * size : (t + 1) * size]
            back = here[:, 2 * CH :]
            if one_later is not None:
                back = back + one_later[:, CH : 2 * CH]
            if two_later is not None:
                back = back + two_later[:, :CH]
            frame = start + t
            grad = x_ref[frame, 1 : 1 + rows, :, CH : 2 * CH].reshape(size, CH).astype(F32)
            new = grad + slope_ref[frame].reshape(size, CH) * back
            emit(frame, new.astype(BF))
            two_later = one_later
            one_later = here


def load(low_ref, own_ref, high_ref, x_ref):
    for t in range(FRAMES):
        whole = jnp.concatenate([low_ref[t], own_ref[t], high_ref[t]], axis=0)
        fill(x_ref, t, 0, whole.reshape(-1, CH).astype(F32))


def emit_to(refs):
    out_ref, top_ref, bottom_ref = refs
    edge = top_ref.shape[1]

    def emit(frame, value):
        whole = value.reshape(ROWS, COLS, CH)
        out_ref[frame] = whole
        top_ref[frame] = whole[:edge]
        bottom_ref[frame] = whole[ROWS - edge :]

    return emit


PIECES = 3


class Stream:
    def __init__(self, source, held, sems):
        size = source.shape[0] // PIECES
        self.held = held
        self.copies = [
            pltpu.make_async_copy(
                source.at[pl.ds(n * size, size)], held.at[pl.ds(n * size, size)], sems.at[n]
            )
            for n in range(PIECES)
        ]
        for copy in self.copies:
            copy.start()

    def get(self):
        for copy in self.copies:
            copy.wait()
        return self.held


def streams(rest, count):
    sources, middle, buffers = rest[:count], rest[count : len(rest) - 2 * count], rest[-2 * count :]
    return middle, [
        Stream(source, buffers[2 * n], buffers[2 * n + 1]) for n, source in enumerate(sources)
    ]


def single_kernel(low_ref, own_ref, high_ref, *rest):
    (*outs, x_ref), (w, slope) = streams(rest, 2)
    load(low_ref, own_ref, high_ref, x_ref)
    back_pass(x_ref, weights(w.get()), slope.get(), ROWS, emit_to(outs))


def last_kernel(low_ref, own_ref, high_ref, *rest):
    (out_ref, x_ref), (w, slope) = streams(rest, 2)
    load(low_ref, own_ref, high_ref, x_ref)

    def emit(frame, value):
        out_ref[frame] = value.reshape(ROWS, COLS, CH)

    back_pass(x_ref, weights(w.get()), slope.get(), ROWS, emit)


def wide_kernel(scale, low_ref, own_ref, high_ref, *rest):
    (own_out, low_out, high_out, part_ref, x_ref), (w, slope, ut) = streams(rest, 3)
    load(low_ref, own_ref, high_ref, x_ref)

    def emit(frame, value):
        whole = value.reshape(ROWS + 2, COLS, CH)
        low_out[frame] = whole[:1]
        own_out[frame] = whole[1 : 1 + ROWS]
        high_out[frame] = whole[1 + ROWS :]

    back_pass(x_ref, weights(w.get()), slope.get(), ROWS + 2, emit)
    tap_terms(ut.get(), own_out[...], scale, part_ref)


def double_kernel(low_ref, own_ref, high_ref, *rest):
    (*outs, middle_ref, x1_ref, x0_ref), (w1, slope1, w0, slope0) = streams(rest, 4)
    load(low_ref, own_ref, high_ref, x1_ref)

    def emit_middle(frame, value):
        fill(x0_ref, frame, 0, value.astype(F32))
        middle_ref[frame] = value.reshape(ROWS + 2, COLS, CH)[1 : 1 + ROWS]

    back_pass(x1_ref, weights(w1.get()), slope1.get(), ROWS + 2, emit_middle)
    back_pass(x0_ref, weights(w0.get()), slope0.get(), ROWS, emit_to(outs))


def tap_terms(ut_ref, grad, scale, out_ref):
    grad = grad.reshape(FRAMES, ROWS * COLS, CH)
    padded = jnp.concatenate([grad, jnp.zeros((2, ROWS * COLS, CH), BF)], axis=0)
    rhs = jnp.concatenate([padded[2 - i : 2 - i + FRAMES] for i in range(3)], axis=-1).reshape(
        FRAMES * ROWS * COLS, 3 * CH
    )
    for n in range(3):
        taps_here = slice(3 * n, 3 * n + 3)
        lhs = ut_ref[taps_here].reshape(3 * CH, FRAMES * ROWS * COLS)
        part = jnp.dot(lhs, rhs, preferred_element_type=F32)
        out_ref[taps_here] = (part * scale).astype(BF).reshape(3, CH, 3 * CH)


def in_vmem(count):
    return [pl.BlockSpec(memory_space=pltpu.VMEM)] * count


def rows_shape(rows):
    return jax.ShapeDtypeStruct((FRAMES, rows, COLS, CH), BF)


PART = jax.ShapeDtypeStruct((9, CH, 3 * CH), BF)


def block_call(kernel, name, operands, streamed, outs, halos):
    scratch = [pltpu.VMEM((FRAMES, r, COLS, 3 * CH), BF) for r in halos]
    for value in streamed:
        scratch += [pltpu.VMEM(value.shape, value.dtype), pltpu.SemaphoreType.DMA((PIECES,))]
    return pl.pallas_call(
        kernel,
        out_shape=[rows_shape(r) if isinstance(r, int) else r for r in outs],
        in_specs=in_vmem(len(operands)) + [pl.BlockSpec(memory_space=pl.ANY)] * len(streamed),
        out_specs=in_vmem(len(outs)),
        scratch_shapes=scratch,
        compiler_params=pltpu.CompilerParams(vmem_limit_bytes=24 << 20),
        name=name,
    )(*operands, *streamed)


def single(low, own, high, w, slope, edge):
    return block_call(
        single_kernel,
        f"one_block_{edge}",
        (low, own, high),
        (w, slope),
        (ROWS, edge, edge),
        (ROWS + 2,),
    )


def last(low, own, high, w, slope):
    return block_call(
        last_kernel, "last_block", (low, own, high), (w, slope), (ROWS,), (ROWS + 2,)
    )[0]


def wide(low, own, high, w, slope, ut, scale):
    return block_call(
        functools.partial(wide_kernel, scale),
        "wide_block",
        (low, own, high),
        (w, slope, ut),
        (ROWS, 1, 1, PART),
        (ROWS + 4,),
    )


def double(low, own, high, w1, slope1, w0, slope0):
    return block_call(
        double_kernel,
        "two_blocks",
        (low, own, high),
        (w1, slope1, w0, slope0),
        (ROWS, 2, 2, ROWS),
        (ROWS + 4, ROWS + 2),
    )


def tap_rows_kernel(act_ref, order_ref, out_ref, u_ref):
    for t in range(FRAMES):
        x = act_ref[t].reshape(-1, CH).astype(F32)
        u = (x * jax.nn.sigmoid(x)).astype(BF).astype(F32)
        col = lax.broadcasted_iota(jnp.int32, u.shape, 0) % COLS
        size = u.shape[0]
        before = jnp.where(col == 0, 0.0, pltpu.roll(u, 1, 0))
        after = jnp.where(col == COLS - 1, 0.0, pltpu.roll(u, size - 1, 0))
        for k, part in enumerate((before, u, after)):
            u_ref[k, t] = part.astype(BF).reshape(ROWS + 2, COLS, CH)
    for j in range(3):
        for k in range(3):
            taken = u_ref[k, :, j : j + ROWS].reshape(FRAMES * ROWS * COLS, CH)
            out_ref[3 * j + k] = lax.dot_general(
                order_ref[...], taken, (((1,), (1,)), ((), ())), preferred_element_type=F32
            ).astype(BF)


def tap_rows(act6, order):
    return pl.pallas_call(
        tap_rows_kernel,
        out_shape=jax.ShapeDtypeStruct((9, CH, FRAMES * ROWS * COLS), BF),
        in_specs=in_vmem(2),
        out_specs=pl.BlockSpec(memory_space=pltpu.VMEM),
        scratch_shapes=[pltpu.VMEM((3, FRAMES, ROWS + 2, COLS, CH), BF)],
        compiler_params=pltpu.CompilerParams(vmem_limit_bytes=24 << 20),
        name="tap_rows",
    )(act6, order)


def taps_kernel(scale, ut_ref, g_ref, more_ref, out_ref):
    tap_terms(ut_ref, g_ref[...] + more_ref[...], scale, out_ref)


def taps(ut, grad, more, scale):
    return pl.pallas_call(
        functools.partial(taps_kernel, scale),
        out_shape=jax.ShapeDtypeStruct((9, CH, 3 * CH), BF),
        in_specs=in_vmem(3),
        out_specs=pl.BlockSpec(memory_space=pltpu.VMEM),
        compiler_params=pltpu.CompilerParams(vmem_limit_bytes=24 << 20),
        name="kernel_taps",
    )(ut, grad, more)


def channel_order():
    share = CH // DP
    order = [
        (chip * 2 + core) * share + rest
        for core in range(2)
        for chip in range(PEERS)
        for rest in range(share)
    ]
    matrix = np.zeros((CH, CH), np.float32)
    matrix[np.arange(CH), order] = 1.0
    return matrix


def slope_of(x):
    x = x.astype(F32)
    sig = jax.nn.sigmoid(x)
    return sig * (1.0 + x * (1.0 - sig))


def local(acts, kernels, cotangent):
    me = lax.axis_index("section")
    dp = lax.axis_index(AXES[1:])
    core = lax.axis_index("core")
    scale = 1.0 / math.sqrt(FRAMES * ROWS * DP * COLS)
    every = range(SEC)
    pairs = (4, 2, 0)
    barrier = lax.optimization_barrier

    def blank(rows):
        return jnp.zeros((FRAMES, rows, COLS, CH), BF)

    both = jnp.concatenate([cotangent, acts[0]], axis=0)
    last_row, first_row, own_acts = barrier((both[:, -1:], both[:, :1], acts[0]))
    edge_low = permute(last_row, [(7, 7, 1)])
    edge_high = permute(first_row, [(7, 7, -1)])
    low0, high0 = edge_low[:FRAMES], edge_high[:FRAMES]

    w = kernels[0].reshape(27 * CH, CH)
    slope = slope_of(acts[0])
    result, top, bottom = lax.cond(
        me == 7,
        lambda: tuple(single(low0, cotangent, high0, w, slope, 1)),
        lambda: (blank(ROWS), blank(1), blank(1)),
    )

    def hop(result, top, bottom, source, target):
        own = permute(result, [(source, target, 0)])
        low = permute(bottom, [(source, target, 1)])
        high = permute(top, [(source, target, -1)])
        return low, own, high

    w_next = permute(w, [(s + 1, s, 0) for s in pairs])

    act_low = edge_low[FRAMES:] + permute(own_acts[:, -1:], [(s, s, 1) for s in range(6)])
    act_high = edge_high[FRAMES:] + permute(own_acts[:, :1], [(s, s, -1) for s in range(6)])
    act6 = jnp.concatenate([act_low, own_acts, act_high], axis=1)
    act_next = permute(act6, [(s + 1, s, 0) for s in pairs])
    row = lax.broadcasted_iota(jnp.int32, act_next.shape, 1) + dp * ROWS - 1
    inside = (row >= 0) & (row < DP * ROWS)
    slope_next = jnp.where(inside, slope_of(act_next), 0.0)

    low, own, high = hop(result, top, bottom, 7, 6)
    result, top, bottom = lax.cond(
        me == 6,
        lambda: tuple(single(low, own, high, w, slope, 2)),
        lambda: (result, blank(2), blank(2)),
    )
    own, result = barrier((own, result))
    grad = jnp.where(me == 7, cotangent, own)

    low, own, high = hop(result, top, bottom, 6, 4)
    grad, low = barrier((grad, low))
    came = own
    for section in (4, 2):
        result, top, bottom, grad = lax.cond(
            me == section,
            lambda low=low, own=own, high=high: tuple(
                double(low, own, high, w_next, slope_next, w, slope)
            ),
            lambda result=result, top=top, bottom=bottom, grad=grad: (
                result,
                top,
                bottom,
                grad,
            ),
        )
        low, own, high = hop(result, top, bottom, section, section - 2)
        if section == 4:
            came = came + own
    own_acts, grad, came = barrier((own_acts, grad, came))
    act_low = act_low + permute(own_acts[:, -1:], [(6, 6, 1)])
    act_high = act_high + permute(own_acts[:, :1], [(6, 6, -1)])
    act6 = jnp.concatenate([act_low, own_acts, act_high], axis=1)
    ut = tap_rows(act6, jnp.asarray(channel_order(), BF))
    ut, grad, low, own, high, came = barrier((ut, grad, low, own, high, came))

    forward = [(s - 1, s, 0) for s in (5, 3, 1)]
    passed = permute(came + own, forward)

    grad, low, high, part = lax.cond(
        me == 0,
        lambda: tuple(wide(low, own, high, w_next, slope_next, ut, scale)),
        lambda: (grad, blank(1), blank(1), jnp.zeros(PART.shape, BF)),
    )
    part = lax.cond(me == 0, lambda: part, lambda: taps(ut, grad, passed, scale))
    final = lax.cond(
        me == 0,
        lambda: last(low, grad, high, w, slope),
        lambda: result,
    )
    final = final + permute(grad, forward)

    half = CH // 2
    keep = lax.dynamic_slice_in_dim(part, core * half, half, 1)
    give = lax.dynamic_slice_in_dim(part, (1 - core) * half, half, 1)
    got = lax.ppermute(
        give, AXES, [(s * DP + d, s * DP + (d ^ 1)) for s in every for d in range(DP)]
    )
    part = (keep.astype(F32) + got.astype(F32)).astype(BF)
    part = jnp.transpose(part.reshape(9, PEERS, CH // DP, 3 * CH), (1, 0, 2, 3))
    part = lax.all_to_all(part, ("z", "y"), 0, 0, tiled=True)
    part = jnp.sum(part.astype(F32), axis=0)
    share = CH // DP
    kernel_part = jnp.transpose(part.reshape(9, share, 3, CH), (1, 2, 0, 3)).reshape(share, 27, CH)
    return (final[None], kernel_part[None])


def solution(mesh):
    parts = Mesh(mesh.devices.reshape(SEC, DP // 4, 2, 2), AXES)
    rows = AXES[1:]
    return jax.shard_map(
        local,
        mesh=parts,
        in_specs=(
            P("section", None, rows, None, None),
            P("section", None, None, None, None, None),
            P(None, rows, None, None),
        ),
        out_specs=(P("section", None, rows, None, None), P("section", rows, None, None)),
        check_vma=False,
    )
```

```python
import functools
import math

import jax
import jax.numpy as jnp
import numpy as np
from jax import lax
from jax.experimental import pallas as pl
from jax.experimental.pallas import tpu as pltpu
from jax.sharding import Mesh
from jax.sharding import PartitionSpec as P

BF = jnp.bfloat16
F32 = jnp.float32
DP = 32
SEC = 8
FRAMES = 9
ROWS = 4
COLS = 32
CH = 128
PEERS = 16
AXES = ("section", "z", "y", "core")


def permute(value, hops):
    pairs = [
        (src * DP + d, dst * DP + d + off)
        for src, dst, off in hops
        for d in range(DP)
        if 0 <= d + off < DP
    ]
    return lax.ppermute(value, AXES, pairs)


def fill(x_ref, frame, row, value):
    count = value.shape[0] // COLS
    col = lax.broadcasted_iota(jnp.int32, value.shape, 0) % COLS
    size = value.shape[0]
    after = jnp.where(col == COLS - 1, 0.0, pltpu.roll(value, size - 1, 0))
    before = jnp.where(col == 0, 0.0, pltpu.roll(value, 1, 0))
    for n, part in enumerate((after, value, before)):
        x_ref[frame, row : row + count, :, n * CH : (n + 1) * CH] = part.astype(BF).reshape(
            count, COLS, CH
        )


def back_pass(x_ref, w_ref, slope_ref, rows, emit):
    group = 3
    size = rows * COLS
    one_later = None
    two_later = None
    for start in range(FRAMES - group, -1, -group):
        lhs = jnp.concatenate(
            [x_ref[start : start + group, 2 - j : 2 - j + rows] for j in range(3)], axis=-1
        ).reshape(group * size, 9 * CH)
        part = jnp.dot(lhs, w_ref[...], preferred_element_type=F32)
        for t in range(group - 1, -1, -1):
            here = part[t * size : (t + 1) * size]
            back = here[:, 2 * CH :]
            if one_later is not None:
                back = back + one_later[:, CH : 2 * CH]
            if two_later is not None:
                back = back + two_later[:, :CH]
            frame = start + t
            grad = x_ref[frame, 1 : 1 + rows, :, CH : 2 * CH].reshape(size, CH).astype(F32)
            new = grad + slope_ref[frame].reshape(size, CH) * back
            emit(frame, new.astype(BF))
            two_later = one_later
            one_later = here


def emit_to(refs):
    out_ref, top_ref, bottom_ref = refs

    def emit(frame, value):
        whole = value.reshape(ROWS, COLS, CH)
        out_ref[frame] = whole
        top_ref[frame] = whole[:2]
        bottom_ref[frame] = whole[2:]

    return emit


def single_kernel(low_ref, own_ref, high_ref, w_ref, slope_ref, *rest):
    *outs, x_ref = rest
    for t in range(FRAMES):
        whole = jnp.concatenate([low_ref[t], own_ref[t], high_ref[t]], axis=0)
        fill(x_ref, t, 0, whole.reshape(-1, CH).astype(F32))
    back_pass(x_ref, w_ref, slope_ref, ROWS, emit_to(outs))


def double_kernel(low_ref, own_ref, high_ref, w1_ref, slope1_ref, w0_ref, slope0_ref, *rest):
    *outs, x1_ref, x0_ref = rest
    for t in range(FRAMES):
        whole = jnp.concatenate([low_ref[t], own_ref[t], high_ref[t]], axis=0)
        fill(x1_ref, t, 0, whole.reshape(-1, CH).astype(F32))

    def emit_mid(frame, value):
        fill(x0_ref, frame, 0, value.astype(F32))

    back_pass(x1_ref, w1_ref, slope1_ref, ROWS + 2, emit_mid)
    back_pass(x0_ref, w0_ref, slope0_ref, ROWS, emit_to(outs))


def in_vmem(count):
    return [pl.BlockSpec(memory_space=pltpu.VMEM)] * count


def gradient_shapes():
    return [
        jax.ShapeDtypeStruct((FRAMES, rows, COLS, CH), BF) for rows in (ROWS, 2, 2)
    ]


def single(low, own, high, w, slope):
    return pl.pallas_call(
        single_kernel,
        out_shape=gradient_shapes(),
        in_specs=in_vmem(5),
        out_specs=in_vmem(3),
        scratch_shapes=[pltpu.VMEM((FRAMES, ROWS + 2, COLS, 3 * CH), BF)],
        compiler_params=pltpu.CompilerParams(vmem_limit_bytes=24 << 20),
        name="one_block",
    )(low, own, high, w, slope)


def double(low, own, high, w1, slope1, w0, slope0):
    return pl.pallas_call(
        double_kernel,
        out_shape=gradient_shapes(),
        in_specs=in_vmem(7),
        out_specs=in_vmem(3),
        scratch_shapes=[
            pltpu.VMEM((FRAMES, ROWS + 4, COLS, 3 * CH), BF),
            pltpu.VMEM((FRAMES, ROWS + 2, COLS, 3 * CH), BF),
        ],
        compiler_params=pltpu.CompilerParams(vmem_limit_bytes=24 << 20),
        name="two_blocks",
    )(low, own, high, w1, slope1, w0, slope0)


def tap_rows_kernel(act_ref, order_ref, out_ref, u_ref):
    for t in range(FRAMES):
        x = act_ref[t].reshape(-1, CH).astype(F32)
        u = (x * jax.nn.sigmoid(x)).astype(BF).astype(F32)
        col = lax.broadcasted_iota(jnp.int32, u.shape, 0) % COLS
        size = u.shape[0]
        before = jnp.where(col == 0, 0.0, pltpu.roll(u, 1, 0))
        after = jnp.where(col == COLS - 1, 0.0, pltpu.roll(u, size - 1, 0))
        for k, part in enumerate((before, u, after)):
            u_ref[k, t] = part.astype(BF).reshape(ROWS + 2, COLS, CH)
    for j in range(3):
        for k in range(3):
            taken = u_ref[k, :, j : j + ROWS].reshape(FRAMES * ROWS * COLS, CH)
            out_ref[3 * j + k] = lax.dot_general(
                order_ref[...], taken, (((1,), (1,)), ((), ())), preferred_element_type=F32
            ).astype(BF)


def tap_rows(act6, order):
    return pl.pallas_call(
        tap_rows_kernel,
        out_shape=jax.ShapeDtypeStruct((9, CH, FRAMES * ROWS * COLS), BF),
        in_specs=in_vmem(2),
        out_specs=pl.BlockSpec(memory_space=pltpu.VMEM),
        scratch_shapes=[pltpu.VMEM((3, FRAMES, ROWS + 2, COLS, CH), BF)],
        compiler_params=pltpu.CompilerParams(vmem_limit_bytes=24 << 20),
        name="tap_rows",
    )(act6, order)


def taps_kernel(scale, ut_ref, g_ref, out_ref):
    grad = g_ref[...].reshape(FRAMES, ROWS * COLS, CH)
    padded = jnp.concatenate([grad, jnp.zeros((2, ROWS * COLS, CH), BF)], axis=0)
    rhs = jnp.concatenate([padded[2 - i : 2 - i + FRAMES] for i in range(3)], axis=-1).reshape(
        FRAMES * ROWS * COLS, 3 * CH
    )
    for n in range(3):
        taps_here = slice(3 * n, 3 * n + 3)
        lhs = ut_ref[taps_here].reshape(3 * CH, FRAMES * ROWS * COLS)
        part = jnp.dot(lhs, rhs, preferred_element_type=F32)
        out_ref[taps_here] = (part * scale).astype(BF).reshape(3, CH, 3 * CH)


def taps(ut, grad, scale):
    return pl.pallas_call(
        functools.partial(taps_kernel, scale),
        out_shape=jax.ShapeDtypeStruct((9, CH, 3 * CH), BF),
        in_specs=in_vmem(2),
        out_specs=pl.BlockSpec(memory_space=pltpu.VMEM),
        compiler_params=pltpu.CompilerParams(vmem_limit_bytes=24 << 20),
        name="kernel_taps",
    )(ut, grad)


def channel_order():
    share = CH // DP
    order = [
        (chip * 2 + core) * share + rest
        for core in range(2)
        for chip in range(PEERS)
        for rest in range(share)
    ]
    matrix = np.zeros((CH, CH), np.float32)
    matrix[np.arange(CH), order] = 1.0
    return matrix


def slope_of(x):
    x = x.astype(F32)
    sig = jax.nn.sigmoid(x)
    return sig * (1.0 + x * (1.0 - sig))


def as_matrix(kern):
    return jnp.transpose(kern, (1, 2, 4, 0, 3)).reshape(9 * CH, 3 * CH)


def local(acts, kernels, cotangent):
    me = lax.axis_index("section")
    dp = lax.axis_index(AXES[1:])
    core = lax.axis_index("core")
    scale = 1.0 / math.sqrt(FRAMES * ROWS * DP * COLS)
    odd = [s for s in range(SEC) if s % 2 == 1]
    every = range(SEC)
    pair = odd[:-1]
    barrier = lax.optimization_barrier

    both = jnp.concatenate([cotangent, acts[0]], axis=0)
    edge_low = permute(both[:, -1:], [(s, s, 1) for s in every])
    edge_high = permute(both[:, :1], [(s, s, -1) for s in every])
    low0, high0 = edge_low[:FRAMES], edge_high[:FRAMES]
    act6 = jnp.concatenate([edge_low[FRAMES:], acts[0], edge_high[FRAMES:]], axis=1)

    w = as_matrix(kernels[0])
    half = w.shape[0] // 2
    w_half = permute(
        lax.dynamic_slice_in_dim(w, core * half, half, 0), [(s + 1, s, 0) for s in pair]
    )
    slope = slope_of(acts[0])
    none = jnp.zeros((FRAMES, 2, COLS, CH), BF)
    state = lax.cond(
        me == 7,
        lambda: tuple(single(low0, cotangent, high0, w, slope)),
        lambda: (cotangent, none, none),
    )

    act6, state = barrier((act6, state))
    act_next = permute(act6, [(s + 1, s, 0) for s in pair])
    w_other = lax.ppermute(
        w_half, AXES, [(s * DP + d, s * DP + (d ^ 1)) for s in pair for d in range(DP)]
    )
    w_next = jnp.where(
        core == 0,
        jnp.concatenate([w_half, w_other], axis=0),
        jnp.concatenate([w_other, w_half], axis=0),
    )
    row = lax.broadcasted_iota(jnp.int32, act_next.shape, 1) + dp * ROWS - 1
    inside = (row >= 0) & (row < DP * ROWS)
    slope_next = jnp.where(inside, slope_of(act_next), 0.0)

    def hop(state, target):
        result, top, bottom = state
        own = permute(result, [(target + 2, target, 0)])
        low = permute(bottom, [(target + 2, target, 1)])
        high = permute(top, [(target + 2, target, -1)])
        return low, own, high

    def stage(state, arrived, section):
        low, own, high = arrived
        return lax.cond(
            me == section,
            lambda: tuple(double(low, own, high, w_next, slope_next, w, slope)),
            lambda: state,
        )

    state = stage(state, hop(state, 5), 5)
    state = stage(state, hop(state, 3), 3)
    act6, state = barrier((act6, state))
    arrived = hop(state, 1)
    act_prev = permute(act6, [(s, (s + 1) % SEC, 0) for s in every])
    ut = tap_rows(act_prev, jnp.asarray(channel_order(), BF))
    ut, arrived = barrier((ut, arrived))
    result, _, _ = stage(state, arrived, 1)

    def even(result, sections):
        hops = [(s + 1, s) for s in sections]
        own = permute(result, [(a, b, 0) for a, b in hops])
        low = permute(result[:, -1:], [(a, b, 1) for a, b in hops])
        high = permute(result[:, :1], [(a, b, -1) for a, b in hops])
        live = functools.reduce(jnp.logical_or, [me == s for s in sections])
        return lax.cond(
            live,
            lambda: single(low, own, high, w, slope)[0],
            lambda: result,
        )

    result = even(result, (6, 4, 2))
    final = even(result, (0,))

    grad = jnp.where(me == 0, cotangent, result)
    part = taps(ut, grad, scale)
    half = CH // 2
    keep = lax.dynamic_slice_in_dim(part, core * half, half, 1)
    give = lax.dynamic_slice_in_dim(part, (1 - core) * half, half, 1)
    got = lax.ppermute(
        give, AXES, [(s * DP + d, s * DP + (d ^ 1)) for s in every for d in range(DP)]
    )
    part = (keep.astype(F32) + got.astype(F32)).astype(BF)
    part = jnp.transpose(part.reshape(9, PEERS, CH // DP, 3 * CH), (1, 0, 2, 3))
    part = lax.all_to_all(part, ("z", "y"), 0, 0, tiled=True)
    part = jnp.sum(part.astype(F32), axis=0)
    part = permute(part.astype(BF), [((s + 1) % SEC, s, 0) for s in every]).astype(F32)
    share = CH // DP
    kernel_part = jnp.transpose(part.reshape(9, share, 3, CH), (1, 2, 0, 3)).reshape(share, 27, CH)
    return (final[None], kernel_part[None])


def solution(mesh):
    parts = Mesh(mesh.devices.reshape(SEC, DP // 4, 2, 2), AXES)
    rows = AXES[1:]
    return jax.shard_map(
        local,
        mesh=parts,
        in_specs=(
            P("section", None, rows, None, None),
            P("section", None, None, None, None, None),
            P(None, rows, None, None),
        ),
        out_specs=(P("section", None, rows, None, None), P("section", rows, None, None)),
        check_vma=False,
    )
```

```python
import functools
import math

import jax
import jax.numpy as jnp
import numpy as np
from jax import lax
from jax.experimental import pallas as pl
from jax.experimental.pallas import tpu as pltpu
from jax.sharding import Mesh
from jax.sharding import PartitionSpec as P

BF = jnp.bfloat16
F32 = jnp.float32
DP = 32
SEC = 8
FRAMES = 9
ROWS = 4
COLS = 32
CH = 128
PEERS = 16
AXES = ("section", "z", "y", "core")


def permute(value, hops):
    pairs = [
        (src * DP + d, dst * DP + d + off)
        for src, dst, off in hops
        for d in range(DP)
        if 0 <= d + off < DP
    ]
    return lax.ppermute(value, AXES, pairs)


def fill(x_ref, frame, row, value):
    count = value.shape[0] // COLS
    col = lax.broadcasted_iota(jnp.int32, value.shape, 0) % COLS
    size = value.shape[0]
    after = jnp.where(col == COLS - 1, 0.0, pltpu.roll(value, size - 1, 0))
    before = jnp.where(col == 0, 0.0, pltpu.roll(value, 1, 0))
    for n, part in enumerate((after, value, before)):
        x_ref[frame, row : row + count, :, n * CH : (n + 1) * CH] = part.astype(BF).reshape(
            count, COLS, CH
        )


def weights(w_ref):
    return jnp.concatenate(
        [
            jnp.concatenate(
                [w_ref[(9 * i + n) * CH : (9 * i + n + 1) * CH, :] for n in range(9)], axis=1
            )
            for i in range(3)
        ],
        axis=0,
    )


def back_pass(x_ref, rhs, slope_ref, rows, emit):
    group = 3
    size = rows * COLS
    one_later = None
    two_later = None
    for start in range(FRAMES - group, -1, -group):
        lhs = jnp.concatenate(
            [x_ref[start : start + group, 2 - j : 2 - j + rows] for j in range(3)], axis=-1
        ).reshape(group * size, 9 * CH)
        part = lax.dot_general(
            lhs, rhs, (((1,), (1,)), ((), ())), preferred_element_type=F32
        )
        for t in range(group - 1, -1, -1):
            here = part[t * size : (t + 1) * size]
            back = here[:, 2 * CH :]
            if one_later is not None:
                back = back + one_later[:, CH : 2 * CH]
            if two_later is not None:
                back = back + two_later[:, :CH]
            frame = start + t
            grad = x_ref[frame, 1 : 1 + rows, :, CH : 2 * CH].reshape(size, CH).astype(F32)
            new = grad + slope_ref[frame].reshape(size, CH) * back
            emit(frame, new.astype(BF))
            two_later = one_later
            one_later = here


def load(low_ref, own_ref, high_ref, x_ref):
    for t in range(FRAMES):
        whole = jnp.concatenate([low_ref[t], own_ref[t], high_ref[t]], axis=0)
        fill(x_ref, t, 0, whole.reshape(-1, CH).astype(F32))


def emit_to(refs):
    out_ref, top_ref, bottom_ref = refs
    edge = top_ref.shape[1]

    def emit(frame, value):
        whole = value.reshape(ROWS, COLS, CH)
        out_ref[frame] = whole
        top_ref[frame] = whole[:edge]
        bottom_ref[frame] = whole[ROWS - edge :]

    return emit


def single_kernel(low_ref, own_ref, high_ref, *rest):
    w_ref, slope_ref, *outs, x_ref = rest
    load(low_ref, own_ref, high_ref, x_ref)
    back_pass(x_ref, weights(w_ref), slope_ref, ROWS, emit_to(outs))


def last_kernel(low_ref, own_ref, high_ref, *rest):
    w_ref, slope_ref, out_ref, x_ref = rest
    load(low_ref, own_ref, high_ref, x_ref)

    def emit(frame, value):
        out_ref[frame] = value.reshape(ROWS, COLS, CH)

    back_pass(x_ref, weights(w_ref), slope_ref, ROWS, emit)


def wide_kernel(scale, low_ref, own_ref, high_ref, *rest):
    w_ref, slope_ref, ut_ref, own_out, low_out, high_out, keep_ref, give_ref, x_ref = rest
    load(low_ref, own_ref, high_ref, x_ref)

    def emit(frame, value):
        whole = value.reshape(ROWS + 2, COLS, CH)
        low_out[frame] = whole[:1]
        own_out[frame] = whole[1 : 1 + ROWS]
        high_out[frame] = whole[1 + ROWS :]

    back_pass(x_ref, weights(w_ref), slope_ref, ROWS + 2, emit)
    tap_terms(ut_ref, own_out[...], scale, keep_ref, give_ref)


def double_kernel(low_ref, own_ref, high_ref, *rest):
    w1_ref, slope1_ref, w0_ref, slope0_ref, *outs, middle_ref, x1_ref, x0_ref = rest
    load(low_ref, own_ref, high_ref, x1_ref)

    def emit_middle(frame, value):
        fill(x0_ref, frame, 0, value.astype(F32))
        middle_ref[frame] = value.reshape(ROWS + 2, COLS, CH)[1 : 1 + ROWS]

    back_pass(x1_ref, weights(w1_ref), slope1_ref, ROWS + 2, emit_middle)
    back_pass(x0_ref, weights(w0_ref), slope0_ref, ROWS, emit_to(outs))


def tap_terms(ut_ref, grad, scale, keep_ref, give_ref):
    grad = grad.reshape(FRAMES, ROWS * COLS, CH)
    padded = jnp.concatenate([grad, jnp.zeros((2, ROWS * COLS, CH), BF)], axis=0)
    rhs = jnp.concatenate([padded[2 - i : 2 - i + FRAMES] for i in range(3)], axis=-1).reshape(
        FRAMES * ROWS * COLS, 3 * CH
    )
    for n in range(3):
        taps_here = slice(3 * n, 3 * n + 3)
        lhs = ut_ref[taps_here].reshape(3 * CH, FRAMES * ROWS * COLS)
        part = jnp.dot(lhs, rhs, preferred_element_type=F32)
        part = (part * scale).astype(BF).reshape(3, CH, 3 * CH)
        keep_ref[taps_here] = part[:, : CH // 2]
        give_ref[taps_here] = part[:, CH // 2 :]


def in_vmem(count):
    return [pl.BlockSpec(memory_space=pltpu.VMEM)] * count


def rows_shape(rows):
    return jax.ShapeDtypeStruct((FRAMES, rows, COLS, CH), BF)


PART = jax.ShapeDtypeStruct((9, CH // 2, 3 * CH), BF)


def block_call(kernel, name, operands, outs, halos):
    scratch = [pltpu.VMEM((FRAMES, r, COLS, 3 * CH), BF) for r in halos]
    return pl.pallas_call(
        kernel,
        out_shape=[rows_shape(r) if isinstance(r, int) else r for r in outs],
        in_specs=in_vmem(len(operands)),
        out_specs=in_vmem(len(outs)),
        scratch_shapes=scratch,
        compiler_params=pltpu.CompilerParams(vmem_limit_bytes=24 << 20),
        name=name,
    )(*operands)


def single(low, own, high, w, slope, edge):
    return block_call(
        single_kernel,
        f"one_block_{edge}",
        (low, own, high, w, slope),
        (ROWS, edge, edge),
        (ROWS + 2,),
    )


def last(low, own, high, w, slope):
    return block_call(
        last_kernel, "last_block", (low, own, high, w, slope), (ROWS,), (ROWS + 2,)
    )[0]


def wide(low, own, high, w, slope, ut, scale):
    return block_call(
        functools.partial(wide_kernel, scale),
        "wide_block",
        (low, own, high, w, slope, ut),
        (ROWS, 1, 1, PART, PART),
        (ROWS + 4,),
    )


def double(low, own, high, w1, slope1, w0, slope0):
    return block_call(
        double_kernel,
        "two_blocks",
        (low, own, high, w1, slope1, w0, slope0),
        (ROWS, 2, 2, ROWS),
        (ROWS + 4, ROWS + 2),
    )


def tap_rows_kernel(act_ref, order_ref, out_ref, u_ref):
    for t in range(FRAMES):
        x = act_ref[t].reshape(-1, CH).astype(F32)
        u = (x * jax.nn.sigmoid(x)).astype(BF).astype(F32)
        col = lax.broadcasted_iota(jnp.int32, u.shape, 0) % COLS
        size = u.shape[0]
        before = jnp.where(col == 0, 0.0, pltpu.roll(u, 1, 0))
        after = jnp.where(col == COLS - 1, 0.0, pltpu.roll(u, size - 1, 0))
        for k, part in enumerate((before, u, after)):
            u_ref[k, t] = part.astype(BF).reshape(ROWS + 2, COLS, CH)
    for j in range(3):
        for k in range(3):
            taken = u_ref[k, :, j : j + ROWS].reshape(FRAMES * ROWS * COLS, CH)
            out_ref[3 * j + k] = lax.dot_general(
                order_ref[...], taken, (((1,), (1,)), ((), ())), preferred_element_type=F32
            ).astype(BF)


def tap_rows(act6, order):
    return pl.pallas_call(
        tap_rows_kernel,
        out_shape=jax.ShapeDtypeStruct((9, CH, FRAMES * ROWS * COLS), BF),
        in_specs=in_vmem(2),
        out_specs=pl.BlockSpec(memory_space=pltpu.VMEM),
        scratch_shapes=[pltpu.VMEM((3, FRAMES, ROWS + 2, COLS, CH), BF)],
        compiler_params=pltpu.CompilerParams(vmem_limit_bytes=24 << 20),
        name="tap_rows",
    )(act6, order)


def taps_kernel(scale, ut_ref, g_ref, more_ref, keep_ref, give_ref):
    tap_terms(ut_ref, g_ref[...] + more_ref[...], scale, keep_ref, give_ref)


def taps(ut, grad, more, scale):
    return pl.pallas_call(
        functools.partial(taps_kernel, scale),
        out_shape=[PART, PART],
        in_specs=in_vmem(3),
        out_specs=in_vmem(2),
        compiler_params=pltpu.CompilerParams(vmem_limit_bytes=24 << 20),
        name="kernel_taps",
    )(ut, grad, more)


def channel_order():
    share = CH // DP
    matrix = np.zeros((2, CH, CH), np.float32)
    for own in range(2):
        order = [
            (chip * 2 + core) * share + rest
            for core in (own, 1 - own)
            for chip in range(PEERS)
            for rest in range(share)
        ]
        matrix[own, np.arange(CH), order] = 1.0
    return matrix


def slope_of(x):
    x = x.astype(F32)
    sig = jax.nn.sigmoid(x)
    return sig * (1.0 + x * (1.0 - sig))


def local(acts, kernels, cotangent):
    me = lax.axis_index("section")
    dp = lax.axis_index(AXES[1:])
    core = lax.axis_index("core")
    scale = 1.0 / math.sqrt(FRAMES * ROWS * DP * COLS)
    every = range(SEC)
    pairs = (4, 2, 0)
    barrier = lax.optimization_barrier

    def blank(rows):
        return jnp.zeros((FRAMES, rows, COLS, CH), BF)

    both = jnp.concatenate([cotangent, acts[0]], axis=0)
    last_row, first_row, own_acts = barrier((both[:, -1:], both[:, :1], acts[0]))
    edge_low = permute(last_row, [(7, 7, 1)])
    edge_high = permute(first_row, [(7, 7, -1)])
    low0, high0 = edge_low[:FRAMES], edge_high[:FRAMES]

    w = kernels[0].reshape(27 * CH, CH)
    slope = slope_of(acts[0])
    result, top, bottom = lax.cond(
        me == 7,
        lambda: tuple(single(low0, cotangent, high0, w, slope, 1)),
        lambda: (blank(ROWS), blank(1), blank(1)),
    )

    def hop(result, top, bottom, source, target):
        own = permute(result, [(source, target, 0)])
        low = permute(bottom, [(source, target, 1)])
        high = permute(top, [(source, target, -1)])
        return low, own, high

    w_next = permute(w, [(s + 1, s, 0) for s in pairs])

    act_low = edge_low[FRAMES:] + permute(own_acts[:, -1:], [(s, s, 1) for s in range(7)])
    act_high = edge_high[FRAMES:] + permute(own_acts[:, :1], [(s, s, -1) for s in range(7)])
    act6 = jnp.concatenate([act_low, own_acts, act_high], axis=1)
    act_next = permute(act6, [(s + 1, s, 0) for s in pairs])
    row = lax.broadcasted_iota(jnp.int32, act_next.shape, 1) + dp * ROWS - 1
    inside = (row >= 0) & (row < DP * ROWS)
    slope_next = jnp.where(inside, slope_of(act_next), 0.0)

    low, own, high = hop(result, top, bottom, 7, 6)
    result, top, bottom = lax.cond(
        me == 6,
        lambda: tuple(single(low, own, high, w, slope, 2)),
        lambda: (result, blank(2), blank(2)),
    )
    own, result = barrier((own, result))
    grad = jnp.where(me == 7, cotangent, own)

    low, own, high = hop(result, top, bottom, 6, 4)
    grad, low = barrier((grad, low))
    came = own
    for section in (4, 2):
        result, top, bottom, grad = lax.cond(
            me == section,
            lambda low=low, own=own, high=high: tuple(
                double(low, own, high, w_next, slope_next, w, slope)
            ),
            lambda result=result, top=top, bottom=bottom, grad=grad: (
                result,
                top,
                bottom,
                grad,
            ),
        )
        low, own, high = hop(result, top, bottom, section, section - 2)
        if section == 4:
            came = came + own
    act6, grad, came = barrier((act6, grad, came))
    both_orders = jnp.asarray(channel_order(), BF)
    ut = tap_rows(act6, jnp.where(core == 0, both_orders[0], both_orders[1]))
    ut, grad, low, own, high, came = barrier((ut, grad, low, own, high, came))

    forward = [(s - 1, s, 0) for s in (5, 3, 1)]
    passed = permute(came + own, forward)

    none = jnp.zeros(PART.shape, BF)
    grad, low, high, keep, give = lax.cond(
        me == 0,
        lambda: tuple(wide(low, own, high, w_next, slope_next, ut, scale)),
        lambda: (grad, blank(1), blank(1), none, none),
    )
    keep, give = lax.cond(
        me == 0, lambda: (keep, give), lambda: tuple(taps(ut, grad, passed, scale))
    )
    final = lax.cond(
        me == 0,
        lambda: last(low, grad, high, w, slope),
        lambda: result,
    )
    final = final + permute(grad, forward)

    got = lax.ppermute(
        give, AXES, [(s * DP + d, s * DP + (d ^ 1)) for s in every for d in range(DP)]
    )
    part = (keep.astype(F32) + got.astype(F32)).astype(BF)
    part = jnp.transpose(part.reshape(9, PEERS, CH // DP, 3 * CH), (1, 0, 2, 3))
    part = lax.all_to_all(part, ("z", "y"), 0, 0, tiled=True)
    part = jnp.sum(part.astype(F32), axis=0)
    share = CH // DP
    kernel_part = jnp.transpose(part.reshape(9, share, 3, CH), (1, 2, 0, 3)).reshape(share, 27, CH)
    return (final[None], kernel_part[None])


def solution(mesh):
    parts = Mesh(mesh.devices.reshape(SEC, DP // 4, 2, 2), AXES)
    rows = AXES[1:]
    return jax.shard_map(
        local,
        mesh=parts,
        in_specs=(
            P("section", None, rows, None, None),
            P("section", None, None, None, None, None),
            P(None, rows, None, None),
        ),
        out_specs=(P("section", None, rows, None, None), P("section", rows, None, None)),
        check_vma=False,
    )
```

```python
import functools
import math

import jax
import jax.numpy as jnp
import numpy as np
from jax import lax
from jax.experimental import pallas as pl
from jax.experimental.pallas import tpu as pltpu
from jax.sharding import Mesh
from jax.sharding import PartitionSpec as P

BF = jnp.bfloat16
F32 = jnp.float32
DP = 32
SEC = 8
FRAMES = 9
ROWS = 4
COLS = 32
CH = 128
PEERS = 16
AXES = ("section", "z", "y", "core")


def permute(value, hops):
    pairs = [
        (src * DP + d, dst * DP + d + off)
        for src, dst, off in hops
        for d in range(DP)
        if 0 <= d + off < DP
    ]
    return lax.ppermute(value, AXES, pairs)


def fill(x_ref, frame, row, value):
    count = value.shape[0] // COLS
    col = lax.broadcasted_iota(jnp.int32, value.shape, 0) % COLS
    size = value.shape[0]
    after = jnp.where(col == COLS - 1, 0.0, pltpu.roll(value, size - 1, 0))
    before = jnp.where(col == 0, 0.0, pltpu.roll(value, 1, 0))
    for n, part in enumerate((after, value, before)):
        x_ref[frame, row : row + count, :, n * CH : (n + 1) * CH] = part.astype(BF).reshape(
            count, COLS, CH
        )


def weights(w_ref):
    return jnp.concatenate(
        [
            jnp.concatenate(
                [w_ref[(9 * i + n) * CH : (9 * i + n + 1) * CH, :] for n in range(9)], axis=1
            )
            for i in range(3)
        ],
        axis=0,
    )


def back_pass(x_ref, rhs, slope_ref, rows, emit):
    group = 3
    size = rows * COLS
    one_later = None
    two_later = None
    for start in range(FRAMES - group, -1, -group):
        lhs = jnp.concatenate(
            [x_ref[start : start + group, 2 - j : 2 - j + rows] for j in range(3)], axis=-1
        ).reshape(group * size, 9 * CH)
        part = lax.dot_general(
            lhs, rhs, (((1,), (1,)), ((), ())), preferred_element_type=F32
        )
        for t in range(group - 1, -1, -1):
            here = part[t * size : (t + 1) * size]
            back = here[:, 2 * CH :]
            if one_later is not None:
                back = back + one_later[:, CH : 2 * CH]
            if two_later is not None:
                back = back + two_later[:, :CH]
            frame = start + t
            grad = x_ref[frame, 1 : 1 + rows, :, CH : 2 * CH].reshape(size, CH).astype(F32)
            new = grad + slope_ref[frame].reshape(size, CH) * back
            emit(frame, new.astype(BF))
            two_later = one_later
            one_later = here


def emit_to(refs):
    out_ref, top_ref, bottom_ref = refs

    def emit(frame, value):
        whole = value.reshape(ROWS, COLS, CH)
        out_ref[frame] = whole
        top_ref[frame] = whole[:2]
        bottom_ref[frame] = whole[2:]

    return emit


def single_kernel(low_ref, own_ref, high_ref, w_ref, slope_ref, *rest):
    *outs, x_ref = rest
    for t in range(FRAMES):
        whole = jnp.concatenate([low_ref[t], own_ref[t], high_ref[t]], axis=0)
        fill(x_ref, t, 0, whole.reshape(-1, CH).astype(F32))
    back_pass(x_ref, weights(w_ref), slope_ref, ROWS, emit_to(outs))


def double_kernel(
    core_ref, low_ref, own_ref, high_ref, half_ref, other_ref, slope1_ref, w0_ref, slope0_ref, *rest
):
    *outs, x1_ref, x0_ref, w1_ref = rest
    half = half_ref.shape[0]
    core = core_ref[0]
    w1_ref[pl.ds(pl.multiple_of(core * half, half), half), :] = half_ref[...]
    w1_ref[pl.ds(pl.multiple_of((1 - core) * half, half), half), :] = other_ref[...]
    for t in range(FRAMES):
        whole = jnp.concatenate([low_ref[t], own_ref[t], high_ref[t]], axis=0)
        fill(x1_ref, t, 0, whole.reshape(-1, CH).astype(F32))

    def emit_mid(frame, value):
        fill(x0_ref, frame, 0, value.astype(F32))

    back_pass(x1_ref, weights(w1_ref), slope1_ref, ROWS + 2, emit_mid)
    back_pass(x0_ref, weights(w0_ref), slope0_ref, ROWS, emit_to(outs))


def in_vmem(count):
    return [pl.BlockSpec(memory_space=pltpu.VMEM)] * count


def gradient_shapes():
    return [
        jax.ShapeDtypeStruct((FRAMES, rows, COLS, CH), BF) for rows in (ROWS, 2, 2)
    ]


def single(low, own, high, w, slope):
    return pl.pallas_call(
        single_kernel,
        out_shape=gradient_shapes(),
        in_specs=in_vmem(5),
        out_specs=in_vmem(3),
        scratch_shapes=[pltpu.VMEM((FRAMES, ROWS + 2, COLS, 3 * CH), BF)],
        compiler_params=pltpu.CompilerParams(vmem_limit_bytes=24 << 20),
        name="one_block",
    )(low, own, high, w, slope)


def double(core, low, own, high, half, other, slope1, w0, slope0):
    return pl.pallas_call(
        double_kernel,
        out_shape=gradient_shapes(),
        in_specs=[pl.BlockSpec(memory_space=pltpu.SMEM)] + in_vmem(8),
        out_specs=in_vmem(3),
        scratch_shapes=[
            pltpu.VMEM((FRAMES, ROWS + 4, COLS, 3 * CH), BF),
            pltpu.VMEM((FRAMES, ROWS + 2, COLS, 3 * CH), BF),
            pltpu.VMEM((27 * CH, CH), BF),
        ],
        compiler_params=pltpu.CompilerParams(vmem_limit_bytes=24 << 20),
        name="two_blocks",
    )(core.reshape(1), low, own, high, half, other, slope1, w0, slope0)


def tap_rows_kernel(act_ref, order_ref, out_ref, u_ref):
    for t in range(FRAMES):
        x = act_ref[t].reshape(-1, CH).astype(F32)
        u = (x * jax.nn.sigmoid(x)).astype(BF).astype(F32)
        col = lax.broadcasted_iota(jnp.int32, u.shape, 0) % COLS
        size = u.shape[0]
        before = jnp.where(col == 0, 0.0, pltpu.roll(u, 1, 0))
        after = jnp.where(col == COLS - 1, 0.0, pltpu.roll(u, size - 1, 0))
        for k, part in enumerate((before, u, after)):
            u_ref[k, t] = part.astype(BF).reshape(ROWS + 2, COLS, CH)
    for j in range(3):
        for k in range(3):
            taken = u_ref[k, :, j : j + ROWS].reshape(FRAMES * ROWS * COLS, CH)
            out_ref[3 * j + k] = lax.dot_general(
                order_ref[...], taken, (((1,), (1,)), ((), ())), preferred_element_type=F32
            ).astype(BF)


def tap_rows(act6, order):
    return pl.pallas_call(
        tap_rows_kernel,
        out_shape=jax.ShapeDtypeStruct((9, CH, FRAMES * ROWS * COLS), BF),
        in_specs=in_vmem(2),
        out_specs=pl.BlockSpec(memory_space=pltpu.VMEM),
        scratch_shapes=[pltpu.VMEM((3, FRAMES, ROWS + 2, COLS, CH), BF)],
        compiler_params=pltpu.CompilerParams(vmem_limit_bytes=24 << 20),
        name="tap_rows",
    )(act6, order)


def taps_kernel(scale, ut_ref, g_ref, out_ref):
    grad = g_ref[...].reshape(FRAMES, ROWS * COLS, CH)
    padded = jnp.concatenate([grad, jnp.zeros((2, ROWS * COLS, CH), BF)], axis=0)
    rhs = jnp.concatenate([padded[2 - i : 2 - i + FRAMES] for i in range(3)], axis=-1).reshape(
        FRAMES * ROWS * COLS, 3 * CH
    )
    for n in range(3):
        taps_here = slice(3 * n, 3 * n + 3)
        lhs = ut_ref[taps_here].reshape(3 * CH, FRAMES * ROWS * COLS)
        part = jnp.dot(lhs, rhs, preferred_element_type=F32)
        out_ref[taps_here] = (part * scale).astype(BF).reshape(3, CH, 3 * CH)


def taps(ut, grad, scale):
    return pl.pallas_call(
        functools.partial(taps_kernel, scale),
        out_shape=jax.ShapeDtypeStruct((9, CH, 3 * CH), BF),
        in_specs=in_vmem(2),
        out_specs=pl.BlockSpec(memory_space=pltpu.VMEM),
        compiler_params=pltpu.CompilerParams(vmem_limit_bytes=24 << 20),
        name="kernel_taps",
    )(ut, grad)


def channel_order():
    share = CH // DP
    order = [
        (chip * 2 + core) * share + rest
        for core in range(2)
        for chip in range(PEERS)
        for rest in range(share)
    ]
    matrix = np.zeros((CH, CH), np.float32)
    matrix[np.arange(CH), order] = 1.0
    return matrix


def slope_of(x):
    x = x.astype(F32)
    sig = jax.nn.sigmoid(x)
    return sig * (1.0 + x * (1.0 - sig))


def local(acts, kernels, cotangent):
    me = lax.axis_index("section")
    dp = lax.axis_index(AXES[1:])
    core = lax.axis_index("core")
    scale = 1.0 / math.sqrt(FRAMES * ROWS * DP * COLS)
    odd = [s for s in range(SEC) if s % 2 == 1]
    every = range(SEC)
    pair = odd[:-1]
    barrier = lax.optimization_barrier

    w = kernels[0].reshape(27 * CH, CH)
    half = w.shape[0] // 2
    w_half = permute(
        lax.dynamic_slice_in_dim(w, core * half, half, 0), [(s + 1, s, 0) for s in pair]
    )

    both = jnp.concatenate([cotangent, acts[0]], axis=0)
    edge_low = permute(both[:, -1:], [(s, s, 1) for s in every])
    edge_high = permute(both[:, :1], [(s, s, -1) for s in every])
    low0, high0 = edge_low[:FRAMES], edge_high[:FRAMES]
    act6 = jnp.concatenate([edge_low[FRAMES:], acts[0], edge_high[FRAMES:]], axis=1)

    slope = slope_of(acts[0])
    none = jnp.zeros((FRAMES, 2, COLS, CH), BF)
    state = lax.cond(
        me == 7,
        lambda: tuple(single(low0, cotangent, high0, w, slope)),
        lambda: (cotangent, none, none),
    )

    def hop(state, target):
        result, top, bottom = state
        own = permute(result, [(target + 2, target, 0)])
        low = permute(bottom, [(target + 2, target, 1)])
        high = permute(top, [(target + 2, target, -1)])
        return low, own, high

    act6, state = barrier((act6, state))
    act_next = permute(act6, [(s + 1, s, 0) for s in pair])
    arrived, w_half = barrier((hop(state, 5), w_half))
    w_other = lax.ppermute(
        w_half, AXES, [(s * DP + d, s * DP + (d ^ 1)) for s in pair for d in range(DP)]
    )
    row = lax.broadcasted_iota(jnp.int32, act_next.shape, 1) + dp * ROWS - 1
    inside = (row >= 0) & (row < DP * ROWS)
    slope_next = jnp.where(inside, slope_of(act_next), 0.0)

    def stage(state, arrived, section):
        low, own, high = arrived
        return lax.cond(
            me == section,
            lambda: tuple(
                double(core, low, own, high, w_half, w_other, slope_next, w, slope)
            ),
            lambda: state,
        )

    def even(result, sections):
        hops = [(s + 1, s) for s in sections]
        own = permute(result, [(a, b, 0) for a, b in hops])
        low = permute(result[:, -1:], [(a, b, 1) for a, b in hops])
        high = permute(result[:, :1], [(a, b, -1) for a, b in hops])
        live = functools.reduce(jnp.logical_or, [me == s for s in sections])
        return lax.cond(
            live,
            lambda: single(low, own, high, w, slope)[0],
            lambda: result,
        )

    state = stage(state, arrived, 5)
    act6, state = barrier((act6, state))
    arrived = hop(state, 3)
    act_prev = permute(act6, [(s, (s + 1) % SEC, 0) for s in every])
    ut = tap_rows(act_prev, jnp.asarray(channel_order(), BF))
    ut, arrived = barrier((ut, arrived))
    state = stage(state, arrived, 3)
    arrived = hop(state, 1)
    result = even(state[0], (6, 4, 2))
    result, arrived = barrier((result, arrived))
    result, _, _ = stage((result, state[1], state[2]), arrived, 1)
    final = even(result, (0,))

    part = taps(ut, jnp.where(me == 0, cotangent, result), scale)
    half = CH // 2
    keep = lax.dynamic_slice_in_dim(part, core * half, half, 1)
    give = lax.dynamic_slice_in_dim(part, (1 - core) * half, half, 1)
    got = lax.ppermute(
        give, AXES, [(s * DP + d, s * DP + (d ^ 1)) for s in every for d in range(DP)]
    )
    part = (keep.astype(F32) + got.astype(F32)).astype(BF)
    part = jnp.transpose(part.reshape(9, PEERS, CH // DP, 3 * CH), (1, 0, 2, 3))
    part = lax.all_to_all(part, ("z", "y"), 0, 0, tiled=True)
    part = jnp.sum(part.astype(F32), axis=0)
    part = permute(part.astype(BF), [((s + 1) % SEC, s, 0) for s in every]).astype(F32)
    share = CH // DP
    kernel_part = jnp.transpose(part.reshape(9, share, 3, CH), (1, 2, 0, 3)).reshape(share, 27, CH)
    return (final[None], kernel_part[None])


def solution(mesh):
    parts = Mesh(mesh.devices.reshape(SEC, DP // 4, 2, 2), AXES)
    rows = AXES[1:]
    return jax.shard_map(
        local,
        mesh=parts,
        in_specs=(
            P("section", None, rows, None, None),
            P("section", None, None, None, None, None),
            P(None, rows, None, None),
        ),
        out_specs=(P("section", None, rows, None, None), P("section", rows, None, None)),
        check_vma=False,
    )
```

```python
import functools
import math

import jax
import jax.numpy as jnp
import numpy as np
from jax import lax
from jax.experimental import pallas as pl
from jax.experimental.pallas import tpu as pltpu
from jax.sharding import Mesh
from jax.sharding import PartitionSpec as P

BF = jnp.bfloat16
F32 = jnp.float32
DP = 32
SEC = 8
FRAMES = 9
ROWS = 4
COLS = 32
CH = 128
PEERS = 16
AXES = ("section", "z", "y", "core")


def permute(value, hops):
    pairs = [
        (src * DP + d, dst * DP + d + off)
        for src, dst, off in hops
        for d in range(DP)
        if 0 <= d + off < DP
    ]
    return lax.ppermute(value, AXES, pairs)


def fill(x_ref, frame, row, value):
    count = value.shape[0] // COLS
    col = lax.broadcasted_iota(jnp.int32, value.shape, 0) % COLS
    size = value.shape[0]
    after = jnp.where(col == COLS - 1, 0.0, pltpu.roll(value, size - 1, 0))
    before = jnp.where(col == 0, 0.0, pltpu.roll(value, 1, 0))
    for n, part in enumerate((after, value, before)):
        x_ref[frame, row : row + count, :, n * CH : (n + 1) * CH] = part.astype(BF).reshape(
            count, COLS, CH
        )


def weights(w_ref):
    return jnp.concatenate(
        [
            jnp.concatenate(
                [w_ref[(9 * i + n) * CH : (9 * i + n + 1) * CH, :] for n in range(9)], axis=1
            )
            for i in range(3)
        ],
        axis=0,
    )


def back_pass(x_ref, rhs, slope_ref, rows, emit):
    group = 3
    size = rows * COLS
    one_later = None
    two_later = None
    for start in range(FRAMES - group, -1, -group):
        lhs = jnp.concatenate(
            [x_ref[start : start + group, 2 - j : 2 - j + rows] for j in range(3)], axis=-1
        ).reshape(group * size, 9 * CH)
        part = lax.dot_general(
            lhs, rhs, (((1,), (1,)), ((), ())), preferred_element_type=F32
        )
        for t in range(group - 1, -1, -1):
            here = part[t * size : (t + 1) * size]
            back = here[:, 2 * CH :]
            if one_later is not None:
                back = back + one_later[:, CH : 2 * CH]
            if two_later is not None:
                back = back + two_later[:, :CH]
            frame = start + t
            grad = x_ref[frame, 1 : 1 + rows, :, CH : 2 * CH].reshape(size, CH).astype(F32)
            new = grad + slope_ref[frame].reshape(size, CH) * back
            emit(frame, new.astype(BF))
            two_later = one_later
            one_later = here


def emit_to(refs):
    out_ref, top_ref, bottom_ref = refs

    def emit(frame, value):
        whole = value.reshape(ROWS, COLS, CH)
        out_ref[frame] = whole
        top_ref[frame] = whole[:2]
        bottom_ref[frame] = whole[2:]

    return emit


def single_kernel(low_ref, own_ref, high_ref, w_ref, slope_ref, *rest):
    *outs, x_ref = rest
    for t in range(FRAMES):
        whole = jnp.concatenate([low_ref[t], own_ref[t], high_ref[t]], axis=0)
        fill(x_ref, t, 0, whole.reshape(-1, CH).astype(F32))
    back_pass(x_ref, weights(w_ref), slope_ref, ROWS, emit_to(outs))


def double_kernel(
    core_ref, low_ref, own_ref, high_ref, half_ref, other_ref, slope1_ref, w0_ref, slope0_ref, *rest
):
    *outs, x1_ref, x0_ref, w1_ref = rest
    half = half_ref.shape[0]
    core = core_ref[0]
    w1_ref[pl.ds(pl.multiple_of(core * half, half), half), :] = half_ref[...]
    w1_ref[pl.ds(pl.multiple_of((1 - core) * half, half), half), :] = other_ref[...]
    for t in range(FRAMES):
        whole = jnp.concatenate([low_ref[t], own_ref[t], high_ref[t]], axis=0)
        fill(x1_ref, t, 0, whole.reshape(-1, CH).astype(F32))

    def emit_mid(frame, value):
        fill(x0_ref, frame, 0, value.astype(F32))

    back_pass(x1_ref, weights(w1_ref), slope1_ref, ROWS + 2, emit_mid)
    back_pass(x0_ref, weights(w0_ref), slope0_ref, ROWS, emit_to(outs))


def in_vmem(count):
    return [pl.BlockSpec(memory_space=pltpu.VMEM)] * count


def gradient_shapes():
    return [
        jax.ShapeDtypeStruct((FRAMES, rows, COLS, CH), BF) for rows in (ROWS, 2, 2)
    ]


def single(low, own, high, w, slope):
    return pl.pallas_call(
        single_kernel,
        out_shape=gradient_shapes(),
        in_specs=in_vmem(5),
        out_specs=in_vmem(3),
        scratch_shapes=[pltpu.VMEM((FRAMES, ROWS + 2, COLS, 3 * CH), BF)],
        compiler_params=pltpu.CompilerParams(vmem_limit_bytes=24 << 20),
        name="one_block",
    )(low, own, high, w, slope)


def double(core, low, own, high, half, other, slope1, w0, slope0):
    return pl.pallas_call(
        double_kernel,
        out_shape=gradient_shapes(),
        in_specs=[pl.BlockSpec(memory_space=pltpu.SMEM)] + in_vmem(8),
        out_specs=in_vmem(3),
        scratch_shapes=[
            pltpu.VMEM((FRAMES, ROWS + 4, COLS, 3 * CH), BF),
            pltpu.VMEM((FRAMES, ROWS + 2, COLS, 3 * CH), BF),
            pltpu.VMEM((27 * CH, CH), BF),
        ],
        compiler_params=pltpu.CompilerParams(vmem_limit_bytes=24 << 20),
        name="two_blocks",
    )(core.reshape(1), low, own, high, half, other, slope1, w0, slope0)


def tap_rows_kernel(act_ref, order_ref, out_ref, u_ref):
    for t in range(FRAMES):
        x = act_ref[t].reshape(-1, CH).astype(F32)
        u = (x * jax.nn.sigmoid(x)).astype(BF).astype(F32)
        col = lax.broadcasted_iota(jnp.int32, u.shape, 0) % COLS
        size = u.shape[0]
        before = jnp.where(col == 0, 0.0, pltpu.roll(u, 1, 0))
        after = jnp.where(col == COLS - 1, 0.0, pltpu.roll(u, size - 1, 0))
        for k, part in enumerate((before, u, after)):
            u_ref[k, t] = part.astype(BF).reshape(ROWS + 2, COLS, CH)
    for j in range(3):
        for k in range(3):
            taken = u_ref[k, :, j : j + ROWS].reshape(FRAMES * ROWS * COLS, CH)
            out_ref[3 * j + k] = lax.dot_general(
                order_ref[...], taken, (((1,), (1,)), ((), ())), preferred_element_type=F32
            ).astype(BF)


def tap_rows(act6, order):
    return pl.pallas_call(
        tap_rows_kernel,
        out_shape=jax.ShapeDtypeStruct((9, CH, FRAMES * ROWS * COLS), BF),
        in_specs=in_vmem(2),
        out_specs=pl.BlockSpec(memory_space=pltpu.VMEM),
        scratch_shapes=[pltpu.VMEM((3, FRAMES, ROWS + 2, COLS, CH), BF)],
        compiler_params=pltpu.CompilerParams(vmem_limit_bytes=24 << 20),
        name="tap_rows",
    )(act6, order)


def taps_kernel(scale, ut_ref, g_ref, out_ref):
    grad = g_ref[...].reshape(FRAMES, ROWS * COLS, CH)
    padded = jnp.concatenate([grad, jnp.zeros((2, ROWS * COLS, CH), BF)], axis=0)
    rhs = jnp.concatenate([padded[2 - i : 2 - i + FRAMES] for i in range(3)], axis=-1).reshape(
        FRAMES * ROWS * COLS, 3 * CH
    )
    for n in range(3):
        taps_here = slice(3 * n, 3 * n + 3)
        lhs = ut_ref[taps_here].reshape(3 * CH, FRAMES * ROWS * COLS)
        part = jnp.dot(lhs, rhs, preferred_element_type=F32)
        out_ref[taps_here] = (part * scale).astype(BF).reshape(3, CH, 3 * CH)


def taps(ut, grad, scale):
    return pl.pallas_call(
        functools.partial(taps_kernel, scale),
        out_shape=jax.ShapeDtypeStruct((9, CH, 3 * CH), BF),
        in_specs=in_vmem(2),
        out_specs=pl.BlockSpec(memory_space=pltpu.VMEM),
        compiler_params=pltpu.CompilerParams(vmem_limit_bytes=24 << 20),
        name="kernel_taps",
    )(ut, grad)


def channel_order():
    share = CH // DP
    order = [
        (chip * 2 + core) * share + rest
        for core in range(2)
        for chip in range(PEERS)
        for rest in range(share)
    ]
    matrix = np.zeros((CH, CH), np.float32)
    matrix[np.arange(CH), order] = 1.0
    return matrix


def slope_of(x):
    x = x.astype(F32)
    sig = jax.nn.sigmoid(x)
    return sig * (1.0 + x * (1.0 - sig))


def local(acts, kernels, cotangent):
    me = lax.axis_index("section")
    dp = lax.axis_index(AXES[1:])
    core = lax.axis_index("core")
    scale = 1.0 / math.sqrt(FRAMES * ROWS * DP * COLS)
    odd = [s for s in range(SEC) if s % 2 == 1]
    every = range(SEC)
    pair = odd[:-1]
    barrier = lax.optimization_barrier

    w = kernels[0].reshape(27 * CH, CH)
    half = w.shape[0] // 2
    w_half = permute(
        lax.dynamic_slice_in_dim(w, core * half, half, 0), [(s + 1, s, 0) for s in pair]
    )

    both = jnp.concatenate([cotangent, acts[0]], axis=0)
    edge_low = permute(both[:, -1:], [(s, s, 1) for s in every])
    edge_high = permute(both[:, :1], [(s, s, -1) for s in every])
    low0, high0 = edge_low[:FRAMES], edge_high[:FRAMES]
    act6 = jnp.concatenate([edge_low[FRAMES:], acts[0], edge_high[FRAMES:]], axis=1)

    slope = slope_of(acts[0])
    none = jnp.zeros((FRAMES, 2, COLS, CH), BF)
    state = lax.cond(
        me == 7,
        lambda: tuple(single(low0, cotangent, high0, w, slope)),
        lambda: (cotangent, none, none),
    )

    def hop(state, target):
        result, top, bottom = state
        own = permute(result, [(target + 2, target, 0)])
        low = permute(bottom, [(target + 2, target, 1)])
        high = permute(top, [(target + 2, target, -1)])
        return low, own, high

    act6, state = barrier((act6, state))
    act_next = permute(act6, [(s + 1, s, 0) for s in pair])
    low5, own5, high5 = hop(state, 5)
    low5, own5, w_half = barrier((low5, own5, w_half))
    arrived = (low5, own5, high5)
    w_other = lax.ppermute(
        w_half, AXES, [(s * DP + d, s * DP + (d ^ 1)) for s in pair for d in range(DP)]
    )
    row = lax.broadcasted_iota(jnp.int32, act_next.shape, 1) + dp * ROWS - 1
    inside = (row >= 0) & (row < DP * ROWS)
    slope_next = jnp.where(inside, slope_of(act_next), 0.0)

    def stage(state, arrived, section):
        low, own, high = arrived
        return lax.cond(
            me == section,
            lambda: tuple(
                double(core, low, own, high, w_half, w_other, slope_next, w, slope)
            ),
            lambda: state,
        )

    def even(result, sections):
        hops = [(s + 1, s) for s in sections]
        own = permute(result, [(a, b, 0) for a, b in hops])
        low = permute(result[:, -1:], [(a, b, 1) for a, b in hops])
        high = permute(result[:, :1], [(a, b, -1) for a, b in hops])
        live = functools.reduce(jnp.logical_or, [me == s for s in sections])
        return lax.cond(
            live,
            lambda: single(low, own, high, w, slope)[0],
            lambda: result,
        )

    state = stage(state, arrived, 5)
    act6, state = barrier((act6, state))
    arrived = hop(state, 3)
    act_prev = permute(act6, [(s, (s + 1) % SEC, 0) for s in every])
    ut = tap_rows(act_prev, jnp.asarray(channel_order(), BF))
    ut, arrived = barrier((ut, arrived))
    state = stage(state, arrived, 3)
    arrived = hop(state, 1)
    result = even(state[0], (6, 4, 2))
    result, arrived = barrier((result, arrived))
    result, _, _ = stage((result, state[1], state[2]), arrived, 1)
    final = even(result, (0,))

    part = taps(ut, jnp.where(me == 0, cotangent, result), scale)
    half = CH // 2
    keep = lax.dynamic_slice_in_dim(part, core * half, half, 1)
    give = lax.dynamic_slice_in_dim(part, (1 - core) * half, half, 1)
    got = lax.ppermute(
        give, AXES, [(s * DP + d, s * DP + (d ^ 1)) for s in every for d in range(DP)]
    )
    part = (keep.astype(F32) + got.astype(F32)).astype(BF)
    part = jnp.transpose(part.reshape(9, PEERS, CH // DP, 3 * CH), (1, 0, 2, 3))
    part = lax.all_to_all(part, ("z", "y"), 0, 0, tiled=True)
    part = jnp.sum(part.astype(F32), axis=0)
    part = permute(part.astype(BF), [((s + 1) % SEC, s, 0) for s in every]).astype(F32)
    share = CH // DP
    kernel_part = jnp.transpose(part.reshape(9, share, 3, CH), (1, 2, 0, 3)).reshape(share, 27, CH)
    return (final[None], kernel_part[None])


def solution(mesh):
    parts = Mesh(mesh.devices.reshape(SEC, DP // 4, 2, 2), AXES)
    rows = AXES[1:]
    return jax.shard_map(
        local,
        mesh=parts,
        in_specs=(
            P("section", None, rows, None, None),
            P("section", None, None, None, None, None),
            P(None, rows, None, None),
        ),
        out_specs=(P("section", None, rows, None, None), P("section", rows, None, None)),
        check_vma=False,
    )
```
